32 devices in a mesh: dom: 8 (over z, y), sub: 4 (over x, core).
Axes of the slice: x: 2, y: 2, z: 4, core: 2. Of those that a mesh axis runs over, the one named last changes fastest.
Arguments:
- modal_state: float32 [56, 9, 4096], P(None, None, ('dom', 'sub')), may hold values from -6 to 6
- star_mats: float32 [3, 9, 9, 4096], P(None, None, None, ('dom', 'sub')), may hold values from -2 to 2
- face_flux: float32 [2, 4, 9, 9, 4096], P(None, None, None, None, ('dom', 'sub')), may hold values from -1.5 to 1.5
- stiffness: float32 [3, 56, 56], replicated, may hold values from -1 to 1
- stiff_vol: float32 [3, 56, 56], replicated, may hold values from -0.5 to 0.5
- face_proj: float32 [4, 56, 21], replicated, may hold values from -0.75 to 0.75
- face_lifting_matrix: float32 [4, 21, 56], replicated, may hold values from -0.625 to 0.625
- orient_maps: float32 [3, 21, 21], replicated, may hold values from -1.25 to 1.25
- neighbours: int32 [4, 4096], P(None, ('dom', 'sub')), may hold values from -1 to 895, as said below
- face_orient: int32 [4, 4096], P(None, ('dom', 'sub')), may hold values from 0 to 2
- send_slots: int32 [2, 1024], P(None, ('dom', 'sub')), may hold values from 0 to 511
- fast_count: int32 [32], P(('dom', 'sub')), may hold values from 1 to 64, as said below
Outputs:
- new_state: float32 [56, 9, 4096], P(None, None, ('dom', 'sub'))
The draws below stay inside these ranges and needn't reach their ends.
Inputs may be any that keep to these rules, and one draw needn't show every extreme that they name: `neighbours`: entry [j, e] is -1 for an absorbing boundary face; below 512 it names a trace of the element's own device; above, it names a send slot of row 0 of a device of the same partition, or of row 1 of a device one partition lower (offset 4 * 32) or one higher (offset 2 * 4 * 32), as in the reference program; the first and last partitions name no missing side. A device's first fast_count elements form its fast cluster. `send_slots`: entry k of a device's row names the own trace that fills its k-th slot.
All inputs are finite; a program needn't handle non-finite values.
Results may differ from the reference program's by a relative error of at most 0.0003.
Values sent between devices are 32-bit elements; how exact they have to be, the bound alone decides.
A program may use at most 64 MiB of HBM per device.

```python
import math
import jax
import jax.numpy as jnp
from jax import lax

MODES = 56
FIELDS = 9
FACE_MODES = 21
DEGREE = 5
ELEM_DEV = 128
SLOTS_PER_UNIT = 32
FAST_MAX = 64
ELEMS = 4096
SLOTS = 1024
N_DOM = 8
N_SUB = 4


def draw_neighbours(key, part):
    device_count = N_DOM * N_SUB
    elem_total = ELEM_DEV * device_count
    local_len = 4 * ELEM_DEV
    group_len = N_SUB * SLOTS_PER_UNIT
    kind_key, local_key, slot_key = jax.random.split(jax.random.fold_in(key, 11), 3)
    kind_pick = jax.random.randint(kind_key, (4, elem_total), 0, 20)
    local_pick = jax.random.randint(local_key, (4, elem_total), 0, local_len)
    slot_pick = jax.random.randint(slot_key, (4, elem_total), 0, group_len)
    dom_index = jnp.arange(elem_total, dtype=jnp.int32) // ELEM_DEV // N_SUB
    lower_ok = (kind_pick >= 14) & (kind_pick < 17) & (dom_index[None, :] > 0)
    upper_ok = (kind_pick >= 17) & (dom_index[None, :] < N_DOM - 1)
    remote = local_len + slot_pick + jnp.where(lower_ok, group_len, 0) + jnp.where(upper_ok, 2 * group_len, 0)
    values = jnp.where(kind_pick == 0, -1, jnp.where(kind_pick <= 10, local_pick, remote))
    values = values.at[0, 0].set(local_len + 3 * group_len - 1)
    values = values.at[3, elem_total - 1].set(-1)
    return values.astype(jnp.int32)


def draw_fast_count(key, part):
    device_count = N_DOM * N_SUB
    base_key, heavy_key, rank_key = jax.random.split(jax.random.fold_in(key, 23), 3)
    base_load = jax.random.randint(base_key, (device_count,), max(1, FAST_MAX // 8), FAST_MAX // 2 + 1)
    heavy_load = jax.random.randint(heavy_key, (device_count,), 0, 16) == 0
    counts = jnp.where(heavy_load, FAST_MAX, base_load)
    busy_rank = jax.random.randint(rank_key, (), 0, device_count)
    return counts.at[busy_rank].set(FAST_MAX).astype(jnp.int32)


def place_ends(values, key, least, top_value):
    dims = values.shape
    index_at = [jax.random.randint(jax.random.fold_in(key, axis), (), 0, dims[axis]) for axis in range(len(dims))]
    values = values.at[tuple(index_at)].set(least)
    longest = dims.index(max(dims))
    index_at[longest] = (index_at[longest] + 1) % dims[longest]
    return values.at[tuple(index_at)].set(top_value)


def block_scale(rng, dims, cuts, smallest, largest):
    loudness, own = 1.0, jax.random.fold_in(rng, 6)
    for axis_at, parts in cuts:
        heights = jnp.exp(jax.random.uniform(jax.random.fold_in(own, axis_at), (parts,), jnp.float32, smallest / len(cuts), largest / len(cuts)))
        loudness = loudness * jnp.repeat(heights, dims[axis_at] // parts).reshape([-1 if axis == axis_at else 1 for axis in range(len(dims))])
    return loudness


def centred(rng, dims, scale, most, cuts=(), kind=jnp.bfloat16):
    values = scale * jax.random.normal(rng, dims, jnp.float32)
    if cuts:
        values = values * block_scale(rng, dims, cuts, -0.22, 0.18)
    return jnp.clip(values, -most, most).astype(kind)


def setup_inputs(seed: int = 0) -> dict:
    keys = jax.random.split(jax.random.key(seed), 13)
    modal_state = centred(keys[0], (MODES, FIELDS, ELEMS), 1.0, 6.0, ((2, 32),), jnp.float32)
    star_mats = centred(keys[1], (3, FIELDS, FIELDS, ELEMS), FIELDS ** -0.5, 2.0, ((3, 32),), jnp.float32)
    face_flux = centred(keys[2], (2, 4, FIELDS, FIELDS, ELEMS), (2 * FIELDS) ** -0.5, 1.5, ((4, 32),), jnp.float32)
    stiffness = centred(keys[3], (3, MODES, MODES), (3 * MODES // 4) ** -0.5, 1.0, (), jnp.float32)
    stiff_vol = centred(keys[4], (3, MODES, MODES), (3 * MODES) ** -0.5, 0.5, (), jnp.float32)
    face_proj = centred(keys[5], (4, MODES, FACE_MODES), MODES ** -0.5, 0.75, (), jnp.float32)
    face_lifting_matrix = centred(keys[6], (4, FACE_MODES, MODES), (4 * FACE_MODES) ** -0.5, 0.625, (), jnp.float32)
    orient_maps = centred(keys[7], (3, FACE_MODES, FACE_MODES), FACE_MODES ** -0.5, 1.25, (), jnp.float32)
    neighbours = draw_neighbours(jax.random.fold_in(keys[12], 71), 0)
    face_orient = place_ends(jax.random.randint(keys[9], (4, ELEMS), 0, 3), jax.random.fold_in(keys[9], 1), 0, 2).astype(jnp.int32)
    send_slots = place_ends(jax.random.randint(keys[10], (2, SLOTS), 0, 4 * ELEM_DEV), jax.random.fold_in(keys[10], 1), 0, (4 * ELEM_DEV) - 1).astype(jnp.int32)
    fast_count = draw_fast_count(jax.random.fold_in(keys[12], 71), 0)
    return dict(modal_state=modal_state, star_mats=star_mats, face_flux=face_flux, stiffness=stiffness, stiff_vol=stiff_vol, face_proj=face_proj, face_lifting_matrix=face_lifting_matrix, orient_maps=orient_maps, neighbours=neighbours, face_orient=face_orient, send_slots=send_slots, fast_count=fast_count)


half_step = 1.0
highest_derivative_order = lax.Precision.HIGHEST


def time_derivative_terms(state, star_mats, stiffness):
    taylor_terms = [state]
    current = state
    for term_order in range(DEGREE):
        mixed_terms = jnp.einsum('dfge,nge->dnfe', star_mats, current, precision=highest_derivative_order)
        current = -jnp.einsum('dmn,dnfe->mfe', stiffness, mixed_terms, precision=highest_derivative_order)
        taylor_terms.append(current)
    return taylor_terms


def integrate(taylor_terms, start, stop):
    running = jnp.zeros_like(taylor_terms[0])
    for term_order, term_value in enumerate(taylor_terms):
        weight = (stop ** (term_order + 1) - start ** (term_order + 1)) / math.factorial(term_order + 1)
        running = running + weight * term_value
    return running


def project(integral, face_proj):
    return jnp.einsum('jmp,mfe->pfje', face_proj, integral, precision=highest_derivative_order)


def update(integral, own_faces, near_faces, star_mats, face_flux, stiff_vol, face_lifting_matrix):
    mixed_terms = jnp.einsum('dfge,nge->dnfe', star_mats, integral, precision=highest_derivative_order)
    volume = jnp.einsum('dmn,dnfe->mfe', stiff_vol, mixed_terms, precision=highest_derivative_order)
    face_contribution_terms = jnp.einsum('jfge,pgje->pfje', face_flux[0], own_faces, precision=highest_derivative_order)
    face_contribution_terms = face_contribution_terms + jnp.einsum('jfge,pgje->pfje', face_flux[1], near_faces, precision=highest_derivative_order)
    lifted_face_modes = jnp.einsum('dlg,lads->gas', face_lifting_matrix, face_contribution_terms, precision=highest_derivative_order)
    return volume - lifted_face_modes


def resolve(nbr_block, device, send_slots):
    local_len = 4 * ELEM_DEV
    group_len = N_SUB * SLOTS_PER_UNIT
    dom_index = device // N_SUB
    offset = jnp.clip(nbr_block - local_len, 0, 3 * group_len - 1)
    group_id = offset // group_len
    within = offset % group_len
    peer_sub = within // SLOTS_PER_UNIT
    slot_index = within % SLOTS_PER_UNIT
    peer_dom = dom_index + jnp.where(group_id == 1, -1, jnp.where(group_id == 2, 1, 0))
    peer_dev = jnp.clip(peer_dom, 0, N_DOM - 1) * N_SUB + peer_sub
    row_pick = jnp.where(group_id == 0, 0, 1)
    peer_face = send_slots[row_pick, peer_dev * SLOTS_PER_UNIT + slot_index]
    is_local = nbr_block < local_len
    src_dev = jnp.where(is_local, device, peer_dev).astype(jnp.int32)
    src_face = jnp.where(is_local, jnp.maximum(nbr_block, 0), peer_face).astype(jnp.int32)
    return src_dev, src_face, nbr_block >= 0


def reference(modal_state, star_mats, face_flux, stiffness, stiff_vol, face_proj, face_lifting_matrix, orient_maps, neighbours, face_orient, send_slots, fast_count):
    device_count = N_DOM * N_SUB
    elem_count = ELEM_DEV

    def blocks(array):
        lead = array.shape[:-1]
        return jnp.moveaxis(array.reshape(lead + (device_count, elem_count)), -2, 0)

    element_state_full = blocks(modal_state)
    star_all = blocks(star_mats)
    flux_all = blocks(face_flux)
    nbr_all = blocks(neighbours)
    orient_all = blocks(face_orient)
    device_ids = jnp.arange(device_count, dtype=jnp.int32)

    def near_traces(flat_traces, nbr_block, orient_block, device):
        src_dev, src_face, present_element_state = resolve(nbr_block, device, send_slots)
        fetched = flat_traces[src_dev, :, :, src_face]
        fetched = jnp.where(present_element_state[:, :, None, None], fetched, 0.0)
        chosen_maps = orient_maps[orient_block]
        return jnp.einsum('jepq,jeqg->pgje', chosen_maps, fetched, precision=highest_derivative_order)

    def first_pass(inputs):
        state, star_block = inputs
        taylor_terms = time_derivative_terms(state, star_block, stiffness)
        first_part = integrate(taylor_terms, 0.0, half_step)
        second_slow = integrate(taylor_terms, half_step, 2.0 * half_step)
        return first_part, second_slow, project(first_part, face_proj)

    first_all, slow_all, traces_first = lax.map(first_pass, (element_state_full, star_all))
    flat_first = traces_first.reshape(device_count, FACE_MODES, FIELDS, 4 * elem_count)

    def second_pass(inputs):
        device, state, star_block, flux_block, nbr_block, orient_block, first_part, second_slow, own_first = inputs
        near_first = near_traces(flat_first, nbr_block, orient_block, device)
        stepped = state + update(first_part, own_first, near_first, star_block, flux_block, stiff_vol, face_lifting_matrix)
        fast_part = integrate(time_derivative_terms(stepped, star_block, stiffness), 0.0, half_step)
        is_fast = jnp.arange(elem_count, dtype=jnp.int32) < fast_count[device]
        second_part = jnp.where(is_fast, fast_part, second_slow)
        return stepped, second_part, project(second_part, face_proj)

    stepped_all, second_all, traces_second = lax.map(second_pass, (device_ids, element_state_full, star_all, flux_all, nbr_all, orient_all, first_all, slow_all, traces_first))
    flat_second = traces_second.reshape(device_count, FACE_MODES, FIELDS, 4 * elem_count)

    def third_pass(inputs):
        device, stepped, star_block, flux_block, nbr_block, orient_block, second_part, own_second = inputs
        near_second = near_traces(flat_second, nbr_block, orient_block, device)
        return stepped + update(second_part, own_second, near_second, star_block, flux_block, stiff_vol, face_lifting_matrix)

    final_all = lax.map(third_pass, (device_ids, stepped_all, star_all, flux_all, nbr_all, orient_all, second_all, traces_second))
    final_all = jnp.moveaxis(final_all, 0, -2)
    return final_all.reshape(MODES, FIELDS, device_count * elem_count)
```

```python
import functools

import jax
import jax.numpy as jnp
from jax import lax
from jax.experimental import pallas as pl
from jax.experimental.pallas import tpu as pltpu
from jax.sharding import PartitionSpec as P

DEGREE = 5
LANES = 128
F32 = jnp.float32
BF16 = jnp.bfloat16


def up(value, multiple):
    return -(-value // multiple) * multiple


def split(x):
    hi = x.astype(BF16)
    return hi, (x - hi.astype(F32)).astype(BF16)


def stacked(x):
    hi, lo = split(x)
    return jnp.concatenate([hi, lo], axis=0)


def dot(a, b):
    return jnp.dot(a, b, preferred_element_type=F32)


def rows3(x, depth):
    low = x - x.astype(BF16).astype(F32)
    rest = depth - 3 * x.shape[0]
    parts = [x, low, x]
    if rest:
        parts.append(jnp.zeros((rest, x.shape[1]), F32))
    return jnp.concatenate(parts, axis=0).astype(BF16)


def twice(x):
    return jnp.concatenate([x, x], axis=0)


def grow(x, rows):
    if rows == x.shape[0]:
        return x
    return jnp.concatenate([x, jnp.zeros((rows - x.shape[0], x.shape[1]), F32)], axis=0)


def row_of(ref, *lead_and_row):
    lead, row = lead_and_row[:-1], lead_and_row[-1]
    return ref[(*lead, pl.ds(row, 1), slice(None))]


def at_columns(rows, columns, test):
    row = lax.broadcasted_iota(jnp.int32, (rows, columns), 0)
    column = lax.broadcasted_iota(jnp.int32, (rows, columns), 1)
    return jnp.where(test(row, column), 1.0, 0.0).astype(BF16)


def shifted(rows, columns, shift):
    return at_columns(rows, columns, lambda row, column: column == row + shift)


def columns3(w, depth):
    hi, lo = split(w)
    inner = w.shape[1]
    first = at_columns(inner, depth, lambda r, c: (c == r) | (c == r + inner))
    return (dot(hi, first) + dot(lo, shifted(inner, depth, 2 * inner))).astype(BF16)


def kernel(
    sizes,
    state_hbm,
    star_hbm,
    flux_hbm,
    stiff_hbm,
    vol_hbm,
    proj_hbm,
    lift_hbm,
    maps_hbm,
    near_idx_ref,
    orient_ref,
    slots_ref,
    count_ref,
    out_ref,
    star_ref,
    flux_ref,
    stiff_ref,
    vol_ref,
    proj_ref,
    lift_ref,
    maps_ref,
    load_sem,
    star_pair,
    y_even,
    y_odd,
    pair_even,
    pair_odd,
    part,
    part_pair,
    taylor,
    slow,
    part_rows,
    trace,
    table,
    near,
    remote,
    pred_w,
    vol_w,
    proj_w,
    own_w,
    near_w,
    hot_local,
    hot_remote,
    hot_send,
    mask,
    send,
    recv,
    send_sem,
    recv_sem,
    forward_sem,
):
    n_dom, n_sub, modes, fields, face_pad, slots = sizes
    faces = 4
    face_modes = maps_ref.shape[1]
    half = LANES // 2
    pairs = (fields + 1) // 2
    depth = pred_w.shape[1]
    mode_pad = up(modes, 16)
    fold = LANES // slots
    table_rows = table.shape[0]
    fold_rows = table_rows // fold
    group = n_sub * slots
    face_rows = faces * face_pad
    own_count = faces * LANES
    loads = [
        pltpu.make_async_copy(source, target, load_sem.at[i])
        for i, (source, target) in enumerate(
            [
                (stiff_hbm, stiff_ref),
                (state_hbm, out_ref),
                (star_hbm, star_ref),
                (proj_hbm, proj_ref),
                (vol_hbm, vol_ref),
                (lift_hbm, lift_ref),
                (maps_hbm, maps_ref),
                (flux_hbm, flux_ref),
            ]
        )
    ]
    for load in loads:
        load.start()
    dom, sub = lax.axis_index("dom"), lax.axis_index("sub")
    has_low, has_high = dom > 0, dom < n_dom - 1

    barrier = pltpu.get_barrier_semaphore()

    def greet(d, s):
        pl.semaphore_signal(
            barrier, inc=1, device_id={"dom": d, "sub": s}, device_id_type=pl.DeviceIdType.MESH
        )

    chips = n_sub // 2
    chip, core = sub // 2, lax.rem(sub, 2)
    sibling = 2 * chip + 1 - core

    greet(dom, sibling)
    for k in range(1, chips):
        greet(dom, 2 * lax.rem(chip + k, chips) + core)

    @pl.when(has_low)
    def _():
        for c in range(chips):
            greet(dom - 1, 2 * c + core)

    @pl.when(has_high)
    def _():
        for c in range(chips):
            greet(dom + 1, 2 * c + core)

    @pl.when(jnp.logical_not(has_low))
    def _():
        recv[:, 1] = jnp.zeros((2, *recv.shape[2:]), F32)

    @pl.when(jnp.logical_not(has_high))
    def _():
        recv[:, 2] = jnp.zeros((2, *recv.shape[2:]), F32)

    def one_hot(row, rows):
        at = lax.broadcasted_iota(jnp.int32, (rows, LANES), 0)
        return jnp.where(at == row, 1.0, 0.0).astype(BF16)

    tiled = dot(
        stacked(grow(slots_ref[...].astype(F32), 8)),
        at_columns(slots, LANES, lambda row, column: column % slots == row),
    )
    tiled = (tiled[:8] + tiled[8:]).astype(jnp.int32)
    for i in range(2):
        hot_send[:, i * LANES : (i + 1) * LANES] = one_hot(tiled[i : i + 1, :], own_count)

    def by_direction(ref):
        rows = jnp.concatenate([ref[d] for d in range(3)], axis=0)
        return grow(rows, pred_w.shape[0])

    def by_face(ref):
        return jnp.concatenate([grow(ref[:, j, :], face_pad) for j in range(faces)], axis=0)

    loads[0].wait()
    pred_w[...] = columns3(-by_direction(stiff_ref), depth)

    chunks = [tuple(range(f, min(f + 2, fields))) for f in range(0, fields, 2)]
    pair_chunks = [tuple(range(i, min(i + 2, pairs))) for i in range(0, pairs, 2)]

    def cols(chunk):
        return slice(chunk[0] * LANES, (chunk[-1] + 1) * LANES)

    def lane(i):
        return slice(i * LANES, (i + 1) * LANES)

    def side_by_side(values):
        return values[0] if len(values) == 1 else jnp.concatenate(values, axis=1)

    def stiff_rows(value):
        return dot(pred_w[...], rows3(value, depth))[: 3 * modes]

    blocks = [(start, min(16, modes - start)) for start in range(0, modes, 16)]

    def contract(source, terms, rows, targets):
        values = [[] for _ in targets]
        for start, count in blocks:
            totals = [[None] * 3 for _ in targets]
            for g in range(terms):
                for d in range(3):
                    first = d * modes + start
                    item = source[first : first + count, lane(g)]
                    for i, f in enumerate(targets):
                        term = row_of(rows, f, g, d) * item
                        total = totals[i][d]
                        totals[i][d] = term if total is None else total + term
            for i, total in enumerate(totals):
                values[i].append(total[0] + total[1] + total[2])
        return [jnp.concatenate(value, axis=0) for value in values]

    low_half = lax.broadcasted_iota(jnp.int32, (modes, LANES), 1) < half

    def pair_up(first, second):
        return jnp.where(low_half, first, pltpu.roll(second, half, 1))

    def contract_pairs(source, chunk):
        targets = [f for i in chunk for f in (2 * i, 2 * i + 1) if f < fields]
        values = contract(source, pairs, star_pair, targets)
        if len(targets) < 2 * len(chunk):
            values.append(jnp.zeros((modes, LANES), F32))
        result = []
        for i in range(len(chunk)):
            even, odd = values[2 * i], values[2 * i + 1]
            result.append(
                jnp.where(low_half, even, odd)
                + pltpu.roll(jnp.where(low_half, odd, even), half, 1)
            )
        return side_by_side(result)

    def project(chunk, value):
        rows = rows3(value, depth)
        part_rows[:, cols(chunk)] = rows
        value = dot(proj_w[...], rows)
        for i, g in enumerate(chunk):
            for j in range(faces):
                trace[j, g * face_modes : g * face_modes + face_pad, :] = value[
                    j * face_pad : (j + 1) * face_pad, lane(i)
                ]

    def flux_rows(side, src, chunk):
        found = [[] for _ in chunk]
        for j in range(faces):
            totals = [None] * len(chunk)
            for g in range(fields):
                item = src[j, g * face_modes : g * face_modes + face_pad, :]
                for i, f in enumerate(chunk):
                    term = row_of(flux_ref, side, f, g, j) * item
                    totals[i] = term if totals[i] is None else totals[i] + term
            for i, total in enumerate(totals):
                found[i].append(total)
        return [jnp.concatenate(value, axis=0) for value in found]

    def add_out(chunk, value):
        for i, f in enumerate(chunk):
            out_ref[f] = out_ref[f] + value[:modes, lane(i)]

    def out_copy(ex, which, target, region, at):
        return pltpu.make_async_remote_copy(
            src_ref=send.at[ex, which],
            dst_ref=recv.at[ex, region, sub],
            send_sem=send_sem.at[ex, region, at],
            recv_sem=recv_sem.at[ex, region, sub],
            device_id=target,
            device_id_type=pl.DeviceIdType.MESH,
        )

    def exchange_copies(ex):
        inner = [out_copy(ex, 0, {"dom": dom, "sub": sibling}, 0, 0)]
        for k in range(1, chips):
            target = {"dom": dom, "sub": 2 * lax.rem(chip + k, chips) + core}
            inner.append(out_copy(ex, 0, target, 0, k))
        lower = [
            out_copy(ex, 1, {"dom": dom - 1, "sub": 2 * c + core}, 2, c) for c in range(chips)
        ]
        upper = [
            out_copy(ex, 1, {"dom": dom + 1, "sub": 2 * c + core}, 1, c) for c in range(chips)
        ]
        return inner, lower, upper

    def arrival(ex, region, s):
        return pltpu.make_async_remote_copy(
            src_ref=send.at[ex, 0],
            dst_ref=recv.at[ex, region, s],
            send_sem=send_sem.at[ex, region, 0],
            recv_sem=recv_sem.at[ex, region, s],
            device_id={"dom": dom, "sub": sub},
            device_id_type=pl.DeviceIdType.MESH,
        )

    def forward(ex, region, s):
        return pltpu.make_async_remote_copy(
            src_ref=recv.at[ex, region, s],
            dst_ref=recv.at[ex, region, s],
            send_sem=forward_sem.at[ex, region, s],
            recv_sem=recv_sem.at[ex, region, s],
            device_id={"dom": dom, "sub": sibling},
            device_id_type=pl.DeviceIdType.MESH,
        )

    def each_region(do, side):
        @pl.when(has_low)
        def _():
            for c in range(chips):
                do(1, 2 * c + side)

        @pl.when(has_high)
        def _():
            for c in range(chips):
                do(2, 2 * c + side)

        for k in range(1, chips):
            do(0, 2 * lax.rem(chip + k, chips) + side)

    section = lax.broadcasted_iota(jnp.int32, (fold_rows, LANES), 1) // slots

    def send_traces(ex):
        for j in range(faces):
            hi, lo = split(trace[j])
            table[:, lane(j)] = hi
            table[:, lane(faces + j)] = lo
        picked = dot(table[...], twice(hot_send[...]))
        for i in range(2):
            packed = picked[:fold_rows, lane(i)]
            for a in range(1, fold):
                packed = jnp.where(
                    section == a, picked[a * fold_rows : (a + 1) * fold_rows, lane(i)], packed
                )
            send[ex, i] = packed
            if i == 0:
                recv[ex, 0, sub] = packed
        if ex == 0:
            pl.semaphore_wait(
                barrier, chips * (1 + has_low.astype(jnp.int32) + has_high.astype(jnp.int32))
            )
        inner, lower, upper = exchange_copies(ex)

        @pl.when(has_low)
        def _():
            for copy in lower:
                copy.start()

        @pl.when(has_high)
        def _():
            for copy in upper:
                copy.start()

        for copy in inner:
            copy.start()

    def own_update():
        for jj in range(0, faces, 2):
            at = slice(jj * LANES, (jj + 2) * LANES)
            found = dot(table[...], twice(hot_local[:, at]))
            near[jj] = found[:, :LANES]
            near[jj + 1] = found[:, LANES:]
        for chunk in chunks:
            y_even[:, cols(chunk)] = dot(vol_w[...], part_rows[:, cols(chunk)])[: 3 * modes]
        for chunk in chunks:
            volume = side_by_side(contract(y_even, fields, star_ref, chunk))
            own = side_by_side(flux_rows(0, trace, chunk))
            add_out(chunk, volume + dot(own_w[...], rows3(own, 3 * face_rows))[:modes])

    def take_arrivals(ex):
        def pass_on(region, s):
            arrival(ex, region, s).wait_recv()
            forward(ex, region, s).start()

        each_region(pass_on, core)
        arrival(ex, 0, sibling).wait_recv()
        each_region(lambda region, s: arrival(ex, region, s).wait_recv(), 1 - core)

        for region in range(3):
            for b in range(n_sub // fold):
                parts = [recv[ex, region, b * fold + i] for i in range(fold)]
                for a in range(fold):
                    value = None
                    for i in range(fold):
                        moved = parts[i]
                        if i != a:
                            moved = pltpu.roll(moved, ((i - a) * slots) % LANES, 1)
                        value = moved if value is None else jnp.where(section == i, moved, value)
                    first = region * group + b * LANES
                    rows = slice(a * fold_rows, (a + 1) * fold_rows)
                    hi, lo = split(value)
                    remote[rows, first : first + LANES] = hi
                    first = first + 3 * group
                    remote[rows, first : first + LANES] = lo

    def near_update():
        for jj in range(0, faces, 2):
            at = slice(jj * LANES, (jj + 2) * LANES)
            found = dot(remote[...], twice(hot_remote[:, at]))
            near[jj] = near[jj] + found[:, :LANES]
            near[jj + 1] = near[jj + 1] + found[:, LANES:]
        masks = [mask[o].astype(BF16) for o in range(3)]
        for chunk in chunks:
            pieces = []
            for value in flux_rows(1, near, chunk):
                hi, lo = split(value)
                hi = [hi * masks[o] for o in range(3)]
                lo = [lo * masks[o] for o in range(3)]
                pieces.append(jnp.concatenate(hi + lo + hi, axis=0))
            add_out(chunk, dot(near_w[...], side_by_side(pieces)))

    def finish_sends(ex):
        inner, lower, upper = exchange_copies(ex)
        for copy in inner:
            copy.wait_send()

        @pl.when(has_low)
        def _():
            for copy in lower:
                copy.wait_send()

        @pl.when(has_high)
        def _():
            for copy in upper:
                copy.wait_send()

        each_region(lambda region, s: forward(ex, region, s).wait_send(), core)

    def prepare_update():
        for j in range(faces):
            row = near_idx_ref[j : j + 1, :]
            hot_local[:, lane(j)] = one_hot(row, own_count)
            hot_remote[:, lane(j)] = one_hot(row - own_count, 3 * group)
            turn = orient_ref[j : j + 1, :]
            for o in range(3):
                mask[o, j * face_pad : (j + 1) * face_pad, :] = jnp.broadcast_to(
                    jnp.where(turn == o, 1.0, 0.0), (face_pad, LANES)
                )
        vol_w[...] = columns3(by_direction(vol_ref), depth)
        same = shifted(mode_pad, modes, 0)
        lift = []
        for value in split(-by_face(lift_ref)):
            lift.append(
                lax.dot_general(same, value, (((1,), (1,)), ((), ())), preferred_element_type=F32)
            )
        hi, lo = lift[0].astype(BF16), lift[1].astype(BF16)
        own_w[:, :face_rows] = hi
        own_w[:, face_rows : 2 * face_rows] = hi
        own_w[:, 2 * face_rows :] = lo
        turned = None
        map_pad = up(face_pad, 16)
        for o in range(3):
            place = at_columns(
                face_modes,
                3 * face_rows,
                lambda row, column: (column // face_rows == o) & (column % face_pad == row),
            )
            both = dot(stacked(grow(maps_ref[o], map_pad)), place)
            term = both[:face_pad] + both[map_pad : map_pad + face_pad]
            turned = term if turned is None else turned + term
        turned = jnp.concatenate([turned] * faces, axis=0)
        row = lax.broadcasted_iota(jnp.int32, turned.shape, 0)
        column = lax.broadcasted_iota(jnp.int32, turned.shape, 1)
        turned = jnp.where(column % face_rows // face_pad == row // face_pad, turned, 0.0)
        turned_hi, turned_lo = split(turned)
        value = dot(hi, turned_hi) + dot(lo, turned_hi) + dot(hi, turned_lo)
        hi, lo = split(value)
        near_w[:, : 3 * face_rows] = hi
        near_w[:, 3 * face_rows : 6 * face_rows] = hi
        near_w[:, 6 * face_rows :] = lo

    def prepare_pairs():
        low = lax.broadcasted_iota(jnp.int32, (8, LANES), 1) < half
        for f in range(fields):
            for i in range(pairs):
                first = grow(star_ref[f, 2 * i], 8)
                if 2 * i + 1 < fields:
                    second = pltpu.roll(grow(star_ref[f, 2 * i + 1], 8), half, 1)
                else:
                    second = jnp.zeros((8, LANES), F32)
                star_pair[f, i] = jnp.where(low, first, second)[:3]

    def sum_slow():
        for f in range(fields):
            total = part[:, lane(f)]
            weight = 1.0
            for k in range(DEGREE):
                weight = weight / (k + 2)
                total = total + ((2.0 ** (k + 2) - 2.0) * weight) * taylor[k, :, lane(f)]
            slow[:, lane(f)] = total

    loads[1].wait()
    for chunk in chunks:
        value = side_by_side([out_ref[f] for f in chunk])
        part[:, cols(chunk)] = value
        y_even[:, cols(chunk)] = stiff_rows(value)
    loads[2].wait()

    def order(k, weight, source, target):
        weight = weight / (k.astype(F32) + 2.0)
        for chunk in chunks:
            value = side_by_side(contract(source, fields, star_ref, chunk))
            taylor[k, :, cols(chunk)] = value
            part[:, cols(chunk)] = part[:, cols(chunk)] + weight * value
            target[:, cols(chunk)] = stiff_rows(value)
        return weight

    def two_orders(k, weight):
        weight = order(2 * k, weight, y_even, y_odd)
        return order(2 * k + 1, weight, y_odd, y_even)

    weight = lax.fori_loop(0, DEGREE // 2, two_orders, jnp.float32(1.0)) / (DEGREE + 1.0)
    loads[3].wait()
    proj_w[...] = columns3(by_face(proj_ref), depth)
    for chunk in chunks:
        value = side_by_side(contract(y_even, fields, star_ref, chunk))
        taylor[DEGREE - 1, :, cols(chunk)] = value
        value = part[:, cols(chunk)] + weight * value
        part[:, cols(chunk)] = value
        project(chunk, value)
    send_traces(0)

    for load in loads[4:]:
        load.wait()
    prepare_update()
    own_update()
    prepare_pairs()
    sum_slow()
    take_arrivals(0)
    near_update()
    finish_sends(0)

    for chunk in pair_chunks:
        value = []
        for i in chunk:
            first = out_ref[2 * i]
            second = out_ref[min(2 * i + 1, fields - 1)]
            value.append(pair_up(first, second))
        value = side_by_side(value)
        part_pair[:, cols(chunk)] = value
        pair_even[:, cols(chunk)] = stiff_rows(value)

    def pair_order(k, weight, source, target):
        weight = weight / (k.astype(F32) + 2.0)
        for chunk in pair_chunks:
            value = contract_pairs(source, chunk)
            part_pair[:, cols(chunk)] = part_pair[:, cols(chunk)] + weight * value
            target[:, cols(chunk)] = stiff_rows(value)
        return weight

    def two_pair_orders(k, weight):
        weight = pair_order(2 * k, weight, pair_even, pair_odd)
        return pair_order(2 * k + 1, weight, pair_odd, pair_even)

    weight = lax.fori_loop(0, DEGREE // 2, two_pair_orders, jnp.float32(1.0)) / (DEGREE + 1.0)
    is_fast = lax.broadcasted_iota(jnp.int32, (modes, LANES), 1) < count_ref[0]
    for chunk in pair_chunks:
        value = part_pair[:, cols(chunk)] + weight * contract_pairs(pair_even, chunk)
        for n, i in enumerate(chunk):
            item = value[:, lane(n)]
            both = [item, pltpu.roll(item, half, 1)]
            mine = tuple(f for f in (2 * i, 2 * i + 1) if f < fields)
            mixed = [
                jnp.where(is_fast, both[q], slow[:, lane(f)]) for q, f in enumerate(mine)
            ]
            project(mine, side_by_side(mixed))
    send_traces(1)
    own_update()
    take_arrivals(1)
    near_update()
    finish_sends(1)


def local(
    n_dom,
    n_sub,
    modal_state,
    star_mats,
    face_flux,
    stiffness,
    stiff_vol,
    face_proj,
    face_lifting_matrix,
    orient_maps,
    neighbours,
    face_orient,
    send_slots,
    fast_count,
):
    modes, fields, elems = modal_state.shape
    face_modes = orient_maps.shape[1]
    slots = send_slots.shape[1]
    fold = LANES // slots
    face_pad, mode_pad = up(face_modes, 8), up(modes, 16)
    table_rows = up((fields - 1) * face_modes + face_pad, 8 * fold)
    group = n_sub * slots
    width = fields * elems
    pairs = (fields + 1) // 2
    depth, rows3 = up(3 * modes, 16), up(3 * modes, 16)
    face_rows = 4 * face_pad
    any_space = pl.BlockSpec(memory_space=pl.ANY)
    vmem = pl.BlockSpec(memory_space=pltpu.VMEM)
    out = pl.pallas_call(
        functools.partial(kernel, (n_dom, n_sub, modes, fields, face_pad, slots)),
        out_shape=jax.ShapeDtypeStruct((fields, modes, elems), F32),
        in_specs=[any_space] * 8 + [vmem] * 3 + [pl.BlockSpec(memory_space=pltpu.SMEM)],
        out_specs=vmem,
        scratch_shapes=[
            pltpu.VMEM((fields, fields, 3, elems), F32),
            pltpu.VMEM((2, fields, fields, 4, elems), F32),
            pltpu.VMEM((3, modes, modes), F32),
            pltpu.VMEM((3, modes, modes), F32),
            pltpu.VMEM((face_modes, 4, modes), F32),
            pltpu.VMEM((face_modes, 4, modes), F32),
            pltpu.VMEM((3, face_modes, face_modes), F32),
            pltpu.SemaphoreType.DMA((8,)),
            pltpu.VMEM((fields, pairs, 3, elems), F32),
            pltpu.VMEM((3 * modes, width), F32),
            pltpu.VMEM((3 * modes, width), F32),
            pltpu.VMEM((3 * modes, pairs * elems), F32),
            pltpu.VMEM((3 * modes, pairs * elems), F32),
            pltpu.VMEM((modes, width), F32),
            pltpu.VMEM((modes, pairs * elems), F32),
            pltpu.VMEM((DEGREE, modes, width), F32),
            pltpu.VMEM((modes, width), F32),
            pltpu.VMEM((depth, width), BF16),
            pltpu.VMEM((4, table_rows, elems), F32),
            pltpu.VMEM((table_rows, 8 * elems), BF16),
            pltpu.VMEM((4, table_rows, elems), F32),
            pltpu.VMEM((table_rows, 6 * group), BF16),
            pltpu.VMEM((rows3, depth), BF16),
            pltpu.VMEM((rows3, depth), BF16),
            pltpu.VMEM((face_rows, depth), BF16),
            pltpu.VMEM((mode_pad, 3 * face_rows), BF16),
            pltpu.VMEM((mode_pad, 9 * face_rows), BF16),
            pltpu.VMEM((4 * elems, 4 * elems), BF16),
            pltpu.VMEM((3 * group, 4 * elems), BF16),
            pltpu.VMEM((4 * elems, 2 * LANES), BF16),
            pltpu.VMEM((3, face_rows, LANES), F32),
            pltpu.VMEM((2, 2, table_rows // fold, LANES), F32),
            pltpu.VMEM((2, 3, n_sub, table_rows // fold, LANES), F32),
            pltpu.SemaphoreType.DMA((2, 3, n_sub)),
            pltpu.SemaphoreType.DMA((2, 3, n_sub)),
            pltpu.SemaphoreType.DMA((2, 3, n_sub)),
        ],
        compiler_params=pltpu.CompilerParams(collective_id=0, has_side_effects=True),
    )(
        modal_state.transpose(1, 0, 2),
        star_mats.transpose(1, 2, 0, 3),
        face_flux.transpose(0, 2, 3, 1, 4),
        stiffness,
        stiff_vol,
        face_proj.transpose(2, 0, 1),
        face_lifting_matrix.transpose(1, 0, 2),
        orient_maps,
        neighbours,
        face_orient,
        send_slots,
        fast_count,
    )
    return out.transpose(1, 0, 2)


def solution(mesh):
    split_last = ("dom", "sub")
    placed = (
        P(None, None, split_last),
        P(None, None, None, split_last),
        P(None, None, None, None, split_last),
        P(),
        P(),
        P(),
        P(),
        P(),
        P(None, split_last),
        P(None, split_last),
        P(None, split_last),
        P(split_last),
    )
    return jax.shard_map(
        functools.partial(local, mesh.shape["dom"], mesh.shape["sub"]),
        mesh=mesh,
        in_specs=placed,
        out_specs=P(None, None, split_last),
        check_vma=False,
    )
```

```python
import functools

import jax
import jax.numpy as jnp
from jax import lax
from jax.experimental import pallas as pl
from jax.experimental.pallas import tpu as pltpu
from jax.sharding import PartitionSpec as P

DEGREE = 5
LANES = 128
F32 = jnp.float32
BF16 = jnp.bfloat16


def up(value, multiple):
    return -(-value // multiple) * multiple


def split(x):
    hi = x.astype(BF16)
    return hi, (x - hi.astype(F32)).astype(BF16)


def stacked(x):
    hi, lo = split(x)
    return jnp.concatenate([hi, lo], axis=0)


def dot(a, b):
    return jnp.dot(a, b, preferred_element_type=F32)


def rows3(x, depth):
    low = x - x.astype(BF16).astype(F32)
    rest = depth - 3 * x.shape[0]
    parts = [x, low, x]
    if rest:
        parts.append(jnp.zeros((rest, x.shape[1]), F32))
    return jnp.concatenate(parts, axis=0).astype(BF16)


def twice(x):
    return jnp.concatenate([x, x], axis=0)


def grow(x, rows):
    if rows == x.shape[0]:
        return x
    return jnp.concatenate([x, jnp.zeros((rows - x.shape[0], x.shape[1]), F32)], axis=0)


def row_of(ref, *lead_and_row):
    lead, row = lead_and_row[:-1], lead_and_row[-1]
    return ref[(*lead, pl.ds(row, 1), slice(None))]


def at_columns(rows, columns, test):
    row = lax.broadcasted_iota(jnp.int32, (rows, columns), 0)
    column = lax.broadcasted_iota(jnp.int32, (rows, columns), 1)
    return jnp.where(test(row, column), 1.0, 0.0).astype(BF16)


def shifted(rows, columns, shift):
    return at_columns(rows, columns, lambda row, column: column == row + shift)


def columns3(w, depth):
    hi, lo = split(w)
    inner = w.shape[1]
    first = at_columns(inner, depth, lambda r, c: (c == r) | (c == r + inner))
    return (dot(hi, first) + dot(lo, shifted(inner, depth, 2 * inner))).astype(BF16)


def kernel(
    sizes,
    state_hbm,
    star_hbm,
    flux_hbm,
    stiff_hbm,
    vol_hbm,
    proj_hbm,
    lift_hbm,
    maps_hbm,
    near_idx_ref,
    orient_ref,
    slots_ref,
    count_ref,
    out_ref,
    star_ref,
    flux_ref,
    stiff_ref,
    vol_ref,
    proj_ref,
    lift_ref,
    maps_ref,
    load_sem,
    star_pair,
    y_even,
    y_odd,
    pair_even,
    pair_odd,
    part,
    part_pair,
    taylor,
    slow,
    part_rows,
    trace,
    table,
    near,
    near_flux,
    remote,
    pred_w,
    vol_w,
    proj_w,
    own_w,
    near_w,
    hot_local,
    hot_remote,
    hot_send,
    mask,
    send_sem,
    recv_sem,
    forward_sem,
    *buffers,
):
    n_dom, n_sub, modes, fields, face_pad, slots = sizes
    faces = 4
    face_modes = maps_ref.shape[1]
    half = LANES // 2
    pairs = (fields + 1) // 2
    depth = pred_w.shape[1]
    mode_pad = up(modes, 16)
    fold = LANES // slots
    pair_chunks = [tuple(range(i, min(i + 2, pairs))) for i in range(0, pairs, 2)]
    parcels = [tuple(f for i in c for f in (2 * i, 2 * i + 1) if f < fields) for c in pair_chunks]
    count = len(parcels)
    sends, recvs = buffers[:count], buffers[count:]
    sizes = [fold * ref.shape[-2] for ref in sends]
    firsts = [sum(sizes[:q]) for q in range(count)]
    field_row = {
        f: firsts[q] + i * face_modes for q, p in enumerate(parcels) for i, f in enumerate(p)
    }
    straight = count - 1
    group = n_sub * slots
    face_rows = faces * face_pad
    own_count = faces * LANES
    loads = [
        pltpu.make_async_copy(source, target, load_sem.at[i])
        for i, (source, target) in enumerate(
            [
                (stiff_hbm, stiff_ref),
                (state_hbm, out_ref),
                (star_hbm, star_ref),
                (proj_hbm, proj_ref),
                (vol_hbm, vol_ref),
                (lift_hbm, lift_ref),
                (maps_hbm, maps_ref),
                (flux_hbm, flux_ref),
            ]
        )
    ]
    for load in loads:
        load.start()
    dom, sub = lax.axis_index("dom"), lax.axis_index("sub")
    has_low, has_high = dom > 0, dom < n_dom - 1

    barrier = pltpu.get_barrier_semaphore()

    def greet(d, s):
        pl.semaphore_signal(
            barrier, inc=1, device_id={"dom": d, "sub": s}, device_id_type=pl.DeviceIdType.MESH
        )

    chips = n_sub // 2
    chip, core = sub // 2, lax.rem(sub, 2)
    sibling = 2 * chip + 1 - core

    for k in range(1, n_sub):
        greet(dom, lax.rem(sub + k, n_sub))

    @pl.when(has_low)
    def _():
        for c in range(n_sub):
            greet(dom - 1, c)

    @pl.when(has_high)
    def _():
        for c in range(n_sub):
            greet(dom + 1, c)

    @pl.when(jnp.logical_not(has_low))
    def _():
        for recv in recvs:
            recv[:, 1] = jnp.zeros((2, *recv.shape[2:]), F32)

    @pl.when(jnp.logical_not(has_high))
    def _():
        for recv in recvs:
            recv[:, 2] = jnp.zeros((2, *recv.shape[2:]), F32)

    for q, fields_of in enumerate(parcels):
        used = firsts[q] + len(fields_of) * face_modes
        end = firsts[q] + sizes[q]
        trace[:, used:end, :] = jnp.zeros((faces, end - used, LANES), F32)

    def one_hot(row, rows):
        at = lax.broadcasted_iota(jnp.int32, (rows, LANES), 0)
        return jnp.where(at == row, 1.0, 0.0).astype(BF16)

    tiled = dot(
        stacked(grow(slots_ref[...].astype(F32), 8)),
        at_columns(slots, LANES, lambda row, column: column % slots == row),
    )
    tiled = (tiled[:8] + tiled[8:]).astype(jnp.int32)
    for i in range(2):
        hot_send[:, i * LANES : (i + 1) * LANES] = one_hot(tiled[i : i + 1, :], own_count)

    def by_direction(ref):
        rows = jnp.concatenate([ref[d] for d in range(3)], axis=0)
        return grow(rows, pred_w.shape[0])

    def by_face(ref):
        return jnp.concatenate([grow(ref[:, j, :], face_pad) for j in range(faces)], axis=0)

    loads[0].wait()
    pred_w[...] = columns3(-by_direction(stiff_ref), depth)

    chunks = [tuple(range(f, min(f + 2, fields))) for f in range(0, fields, 2)]

    def cols(chunk):
        return slice(chunk[0] * LANES, (chunk[-1] + 1) * LANES)

    def lane(i):
        return slice(i * LANES, (i + 1) * LANES)

    def side_by_side(values):
        return values[0] if len(values) == 1 else jnp.concatenate(values, axis=1)

    def stiff_rows(value):
        return dot(pred_w[...], rows3(value, depth))[: 3 * modes]

    blocks = [(start, min(16, modes - start)) for start in range(0, modes, 16)]

    def contract(source, terms, rows, targets):
        values = [[] for _ in targets]
        for start, count in blocks:
            totals = [[None] * 3 for _ in targets]
            for g in range(terms):
                for d in range(3):
                    first = d * modes + start
                    item = source[first : first + count, lane(g)]
                    for i, f in enumerate(targets):
                        term = row_of(rows, f, g, d) * item
                        total = totals[i][d]
                        totals[i][d] = term if total is None else total + term
            for i, total in enumerate(totals):
                values[i].append(total[0] + total[1] + total[2])
        return [jnp.concatenate(value, axis=0) for value in values]

    low_half = lax.broadcasted_iota(jnp.int32, (modes, LANES), 1) < half

    def pair_up(first, second):
        return jnp.where(low_half, first, pltpu.roll(second, half, 1))

    def contract_pairs(source, chunk):
        targets = [f for i in chunk for f in (2 * i, 2 * i + 1) if f < fields]
        values = contract(source, pairs, star_pair, targets)
        if len(targets) < 2 * len(chunk):
            values.append(jnp.zeros((modes, LANES), F32))
        result = []
        for i in range(len(chunk)):
            even, odd = values[2 * i], values[2 * i + 1]
            result.append(
                jnp.where(low_half, even, odd)
                + pltpu.roll(jnp.where(low_half, odd, even), half, 1)
            )
        return side_by_side(result)

    def project(chunk, value):
        rows = rows3(value, depth)
        part_rows[:, cols(chunk)] = rows
        value = dot(proj_w[...], rows)
        for i, g in enumerate(chunk):
            for j in range(faces):
                trace[j, field_row[g] : field_row[g] + face_pad, :] = value[
                    j * face_pad : (j + 1) * face_pad, lane(i)
                ]

    def flux_rows(side, src, chunk, given, starts=None):
        found = [[] for _ in chunk]
        for j in range(faces):
            block = slice(j * face_pad, (j + 1) * face_pad)
            totals = [None if starts is None else starts[f, block, :] for f in chunk]
            for g in given:
                item = src[j, field_row[g] : field_row[g] + face_pad, :]
                for i, f in enumerate(chunk):
                    term = row_of(flux_ref, side, f, g, j) * item
                    totals[i] = term if totals[i] is None else totals[i] + term
            for i, total in enumerate(totals):
                found[i].append(total)
        return [jnp.concatenate(value, axis=0) for value in found]

    def add_out(chunk, value):
        for i, f in enumerate(chunk):
            out_ref[f] = out_ref[f] + value[:modes, lane(i)]

    def out_copy(ex, q, which, target, region, at):
        return pltpu.make_async_remote_copy(
            src_ref=sends[q].at[ex, which],
            dst_ref=recvs[q].at[ex, region, sub],
            send_sem=send_sem.at[ex, q, region, at],
            recv_sem=recv_sem.at[ex, q, region, sub],
            device_id=target,
            device_id_type=pl.DeviceIdType.MESH,
        )

    def exchange_copies(ex, q):
        if q == straight:
            inner = [
                out_copy(ex, q, 0, {"dom": dom, "sub": lax.rem(sub + k, n_sub)}, 0, k)
                for k in range(1, n_sub)
            ]
            beside = [(c, c) for c in range(n_sub)]
        else:
            inner = [out_copy(ex, q, 0, {"dom": dom, "sub": sibling}, 0, 0)]
            for k in range(1, chips):
                target = {"dom": dom, "sub": 2 * lax.rem(chip + k, chips) + core}
                inner.append(out_copy(ex, q, 0, target, 0, k))
            beside = [(2 * c + core, c) for c in range(chips)]
        lower = [out_copy(ex, q, 1, {"dom": dom - 1, "sub": s}, 2, at) for s, at in beside]
        upper = [out_copy(ex, q, 1, {"dom": dom + 1, "sub": s}, 1, at) for s, at in beside]
        return inner, lower, upper

    def arrival(ex, q, region, s):
        return pltpu.make_async_remote_copy(
            src_ref=sends[q].at[ex, 0],
            dst_ref=recvs[q].at[ex, region, s],
            send_sem=send_sem.at[ex, q, region, 0],
            recv_sem=recv_sem.at[ex, q, region, s],
            device_id={"dom": dom, "sub": sub},
            device_id_type=pl.DeviceIdType.MESH,
        )

    def forward(ex, q, region, s):
        return pltpu.make_async_remote_copy(
            src_ref=recvs[q].at[ex, region, s],
            dst_ref=recvs[q].at[ex, region, s],
            send_sem=forward_sem.at[ex, q, region, s],
            recv_sem=recv_sem.at[ex, q, region, s],
            device_id={"dom": dom, "sub": sibling},
            device_id_type=pl.DeviceIdType.MESH,
        )

    def each_region(do, side):
        for k in range(1, chips):
            do(0, 2 * lax.rem(chip + k, chips) + side)

        @pl.when(has_low)
        def _():
            for c in range(chips):
                do(1, 2 * c + side)

        @pl.when(has_high)
        def _():
            for c in range(chips):
                do(2, 2 * c + side)

    def gather(ex, q):
        rows = slice(firsts[q], firsts[q] + sizes[q])
        for j in range(faces):
            hi, lo = split(trace[j, rows, :])
            table[rows, lane(j)] = hi
            table[rows, lane(faces + j)] = lo
        picked = dot(table[rows, :], twice(hot_send[...]))
        fold_rows = sizes[q] // fold
        section = lax.broadcasted_iota(jnp.int32, (fold_rows, LANES), 1) // slots
        for i in range(2):
            packed = picked[:fold_rows, lane(i)]
            for a in range(1, fold):
                packed = jnp.where(
                    section == a, picked[a * fold_rows : (a + 1) * fold_rows, lane(i)], packed
                )
            sends[q][ex, i] = packed
            if i == 0:
                recvs[q][ex, 0, sub] = packed

    def start(ex, q):
        if ex == 0 and q == 0:
            sides = has_low.astype(jnp.int32) + has_high.astype(jnp.int32)
            pl.semaphore_wait(barrier, n_sub - 1 + n_sub * sides)
        inner, lower, upper = exchange_copies(ex, q)

        @pl.when(has_low)
        def _():
            for copy in lower:
                copy.start()

        @pl.when(has_high)
        def _():
            for copy in upper:
                copy.start()

        for copy in inner:
            copy.start()

    def own_update():
        for jj in range(0, faces, 2):
            at = slice(jj * LANES, (jj + 2) * LANES)
            found = dot(table[...], twice(hot_local[:, at]))
            near[jj] = found[:, :LANES]
            near[jj + 1] = found[:, LANES:]
        for chunk in chunks:
            y_even[:, cols(chunk)] = dot(vol_w[...], part_rows[:, cols(chunk)])[: 3 * modes]
        for chunk in chunks:
            volume = side_by_side(contract(y_even, fields, star_ref, chunk))
            own = side_by_side(flux_rows(0, trace, chunk, range(fields)))
            add_out(chunk, volume + dot(own_w[...], rows3(own, 3 * face_rows))[:modes])

    def unpack(ex, q):
        fold_rows = sizes[q] // fold
        section = lax.broadcasted_iota(jnp.int32, (fold_rows, LANES), 1) // slots
        for region in range(3):
            for b in range(n_sub // fold):
                parts = [recvs[q][ex, region, b * fold + i] for i in range(fold)]
                for a in range(fold):
                    value = None
                    for i in range(fold):
                        moved = parts[i]
                        if i != a:
                            moved = pltpu.roll(moved, ((i - a) * slots) % LANES, 1)
                        value = moved if value is None else jnp.where(section == i, moved, value)
                    first = region * group + b * LANES
                    rows = slice(firsts[q] + a * fold_rows, firsts[q] + (a + 1) * fold_rows)
                    remote[rows, first : first + LANES] = value

    def add_near(q):
        rows = slice(firsts[q], firsts[q] + sizes[q])
        hi, lo = split(remote[rows, :])
        both = jnp.concatenate([hi, lo], axis=1)
        for jj in range(0, faces, 2):
            at = slice(jj * LANES, (jj + 2) * LANES)
            found = dot(both, twice(hot_remote[:, at]))
            near[jj, rows, :] = near[jj, rows, :] + found[:, :LANES]
            near[jj + 1, rows, :] = near[jj + 1, rows, :] + found[:, LANES:]

    def near_update(ex):
        for q in range(straight):
            def pass_on(region, s, q=q):
                arrival(ex, q, region, s).wait_recv()
                forward(ex, q, region, s).start()

            each_region(pass_on, core)
        for q in range(count):
            arrival(ex, q, 0, sibling).wait_recv()
            if q == straight:
                each_region(lambda region, s: arrival(ex, q, region, s).wait_recv(), core)
            each_region(lambda region, s: arrival(ex, q, region, s).wait_recv(), 1 - core)
            unpack(ex, q)
            add_near(q)
            starts = near_flux if q else None
            if q < straight:
                for chunk in chunks:
                    for f, value in zip(chunk, flux_rows(1, near, chunk, parcels[q], starts)):
                        near_flux[f] = value
        masks = [mask[o].astype(BF16) for o in range(3)]
        for chunk in chunks:
            pieces = []
            for value in flux_rows(1, near, chunk, parcels[straight], near_flux):
                hi, lo = split(value)
                hi = [hi * masks[o] for o in range(3)]
                lo = [lo * masks[o] for o in range(3)]
                pieces.append(jnp.concatenate(hi + lo + hi, axis=0))
            add_out(chunk, dot(near_w[...], side_by_side(pieces)))

    def finish_sends(ex):
        for q in range(count):
            inner, lower, upper = exchange_copies(ex, q)
            for copy in inner:
                copy.wait_send()

            @pl.when(has_low)
            def _():
                for copy in lower:
                    copy.wait_send()

            @pl.when(has_high)
            def _():
                for copy in upper:
                    copy.wait_send()

            if q < straight:
                each_region(lambda region, s: forward(ex, q, region, s).wait_send(), core)

    def prepare_update():
        for j in range(faces):
            row = near_idx_ref[j : j + 1, :]
            hot_local[:, lane(j)] = one_hot(row, own_count)
            hot_remote[:, lane(j)] = one_hot(row - own_count, 3 * group)
            turn = orient_ref[j : j + 1, :]
            for o in range(3):
                mask[o, j * face_pad : (j + 1) * face_pad, :] = jnp.broadcast_to(
                    jnp.where(turn == o, 1.0, 0.0), (face_pad, LANES)
                )
        vol_w[...] = columns3(by_direction(vol_ref), depth)
        same = shifted(mode_pad, modes, 0)
        lift = []
        for value in split(-by_face(lift_ref)):
            lift.append(
                lax.dot_general(same, value, (((1,), (1,)), ((), ())), preferred_element_type=F32)
            )
        hi, lo = lift[0].astype(BF16), lift[1].astype(BF16)
        own_w[:, :face_rows] = hi
        own_w[:, face_rows : 2 * face_rows] = hi
        own_w[:, 2 * face_rows :] = lo
        turned = None
        map_pad = up(face_pad, 16)
        for o in range(3):
            place = at_columns(
                face_modes,
                3 * face_rows,
                lambda row, column: (column // face_rows == o) & (column % face_pad == row),
            )
            both = dot(stacked(grow(maps_ref[o], map_pad)), place)
            term = both[:face_pad] + both[map_pad : map_pad + face_pad]
            turned = term if turned is None else turned + term
        turned = jnp.concatenate([turned] * faces, axis=0)
        row = lax.broadcasted_iota(jnp.int32, turned.shape, 0)
        column = lax.broadcasted_iota(jnp.int32, turned.shape, 1)
        turned = jnp.where(column % face_rows // face_pad == row // face_pad, turned, 0.0)
        turned_hi, turned_lo = split(turned)
        value = dot(hi, turned_hi) + dot(lo, turned_hi) + dot(hi, turned_lo)
        hi, lo = split(value)
        near_w[:, : 3 * face_rows] = hi
        near_w[:, 3 * face_rows : 6 * face_rows] = hi
        near_w[:, 6 * face_rows :] = lo

    def prepare_pairs():
        low = lax.broadcasted_iota(jnp.int32, (8, LANES), 1) < half
        for f in range(fields):
            for i in range(pairs):
                first = grow(star_ref[f, 2 * i], 8)
                if 2 * i + 1 < fields:
                    second = pltpu.roll(grow(star_ref[f, 2 * i + 1], 8), half, 1)
                else:
                    second = jnp.zeros((8, LANES), F32)
                star_pair[f, i] = jnp.where(low, first, second)[:3]

    def sum_slow():
        for f in range(fields):
            total = part[:, lane(f)]
            weight = 1.0
            for k in range(DEGREE):
                weight = weight / (k + 2)
                total = total + ((2.0 ** (k + 2) - 2.0) * weight) * taylor[k, :, lane(f)]
            slow[:, lane(f)] = total

    loads[1].wait()
    for chunk in chunks:
        value = side_by_side([out_ref[f] for f in chunk])
        part[:, cols(chunk)] = value
        y_even[:, cols(chunk)] = stiff_rows(value)
    loads[2].wait()

    def order(k, weight, source, target):
        weight = weight / (k.astype(F32) + 2.0)
        for chunk in chunks:
            value = side_by_side(contract(source, fields, star_ref, chunk))
            taylor[k, :, cols(chunk)] = value
            part[:, cols(chunk)] = part[:, cols(chunk)] + weight * value
            target[:, cols(chunk)] = stiff_rows(value)
        return weight

    def two_orders(k, weight):
        weight = order(2 * k, weight, y_even, y_odd)
        return order(2 * k + 1, weight, y_odd, y_even)

    weight = lax.fori_loop(0, DEGREE // 2, two_orders, jnp.float32(1.0)) / (DEGREE + 1.0)
    loads[3].wait()
    proj_w[...] = columns3(by_face(proj_ref), depth)
    ready = []
    for chunk in chunks:
        value = side_by_side(contract(y_even, fields, star_ref, chunk))
        taylor[DEGREE - 1, :, cols(chunk)] = value
        value = part[:, cols(chunk)] + weight * value
        part[:, cols(chunk)] = value
        project(chunk, value)
        for q in ready:
            start(0, q)
        ready = [q for q, p in enumerate(parcels) if p[-1] == chunk[-1]]
        for q in ready:
            gather(0, q)
    for q in ready:
        start(0, q)

    for load in loads[4:]:
        load.wait()
    prepare_update()
    own_update()
    prepare_pairs()
    sum_slow()
    near_update(0)
    finish_sends(0)

    for chunk in pair_chunks:
        value = []
        for i in chunk:
            first = out_ref[2 * i]
            second = out_ref[min(2 * i + 1, fields - 1)]
            value.append(pair_up(first, second))
        value = side_by_side(value)
        part_pair[:, cols(chunk)] = value
        pair_even[:, cols(chunk)] = stiff_rows(value)

    def pair_order(k, weight, source, target):
        weight = weight / (k.astype(F32) + 2.0)
        for chunk in pair_chunks:
            value = contract_pairs(source, chunk)
            part_pair[:, cols(chunk)] = part_pair[:, cols(chunk)] + weight * value
            target[:, cols(chunk)] = stiff_rows(value)
        return weight

    def two_pair_orders(k, weight):
        weight = pair_order(2 * k, weight, pair_even, pair_odd)
        return pair_order(2 * k + 1, weight, pair_odd, pair_even)

    weight = lax.fori_loop(0, DEGREE // 2, two_pair_orders, jnp.float32(1.0)) / (DEGREE + 1.0)
    is_fast = lax.broadcasted_iota(jnp.int32, (modes, LANES), 1) < count_ref[0]
    for q, chunk in enumerate(pair_chunks):
        value = part_pair[:, cols(chunk)] + weight * contract_pairs(pair_even, chunk)
        for n, i in enumerate(chunk):
            item = value[:, lane(n)]
            both = [item, pltpu.roll(item, half, 1)]
            mine = tuple(f for f in (2 * i, 2 * i + 1) if f < fields)
            mixed = [
                jnp.where(is_fast, both[q], slow[:, lane(f)]) for q, f in enumerate(mine)
            ]
            project(mine, side_by_side(mixed))
        if q:
            start(1, q - 1)
        gather(1, q)
    start(1, straight)
    own_update()
    near_update(1)
    finish_sends(1)


def local(
    n_dom,
    n_sub,
    modal_state,
    star_mats,
    face_flux,
    stiffness,
    stiff_vol,
    face_proj,
    face_lifting_matrix,
    orient_maps,
    neighbours,
    face_orient,
    send_slots,
    fast_count,
):
    modes, fields, elems = modal_state.shape
    face_modes = orient_maps.shape[1]
    slots = send_slots.shape[1]
    fold = LANES // slots
    face_pad, mode_pad = up(face_modes, 8), up(modes, 16)
    group = n_sub * slots
    width = fields * elems
    pairs = (fields + 1) // 2
    depth, rows3 = up(3 * modes, 16), up(3 * modes, 16)
    face_rows = 4 * face_pad
    parcels = [min(4, fields - f) for f in range(0, fields, 4)]
    rows_of = [up((p - 1) * face_modes + face_pad, 8 * fold) for p in parcels]
    table_rows = sum(rows_of)
    any_space = pl.BlockSpec(memory_space=pl.ANY)
    vmem = pl.BlockSpec(memory_space=pltpu.VMEM)
    out = pl.pallas_call(
        functools.partial(kernel, (n_dom, n_sub, modes, fields, face_pad, slots)),
        out_shape=jax.ShapeDtypeStruct((fields, modes, elems), F32),
        in_specs=[any_space] * 8 + [vmem] * 3 + [pl.BlockSpec(memory_space=pltpu.SMEM)],
        out_specs=vmem,
        scratch_shapes=[
            pltpu.VMEM((fields, fields, 3, elems), F32),
            pltpu.VMEM((2, fields, fields, 4, elems), F32),
            pltpu.VMEM((3, modes, modes), F32),
            pltpu.VMEM((3, modes, modes), F32),
            pltpu.VMEM((face_modes, 4, modes), F32),
            pltpu.VMEM((face_modes, 4, modes), F32),
            pltpu.VMEM((3, face_modes, face_modes), F32),
            pltpu.SemaphoreType.DMA((8,)),
            pltpu.VMEM((fields, pairs, 3, elems), F32),
            pltpu.VMEM((3 * modes, width), F32),
            pltpu.VMEM((3 * modes, width), F32),
            pltpu.VMEM((3 * modes, pairs * elems), F32),
            pltpu.VMEM((3 * modes, pairs * elems), F32),
            pltpu.VMEM((modes, width), F32),
            pltpu.VMEM((modes, pairs * elems), F32),
            pltpu.VMEM((DEGREE, modes, width), F32),
            pltpu.VMEM((modes, width), F32),
            pltpu.VMEM((depth, width), BF16),
            pltpu.VMEM((4, table_rows, elems), F32),
            pltpu.VMEM((table_rows, 8 * elems), BF16),
            pltpu.VMEM((4, table_rows, elems), F32),
            pltpu.VMEM((fields, face_rows, elems), F32),
            pltpu.VMEM((table_rows, 3 * group), F32),
            pltpu.VMEM((rows3, depth), BF16),
            pltpu.VMEM((rows3, depth), BF16),
            pltpu.VMEM((face_rows, depth), BF16),
            pltpu.VMEM((mode_pad, 3 * face_rows), BF16),
            pltpu.VMEM((mode_pad, 9 * face_rows), BF16),
            pltpu.VMEM((4 * elems, 4 * elems), BF16),
            pltpu.VMEM((3 * group, 4 * elems), BF16),
            pltpu.VMEM((4 * elems, 2 * LANES), BF16),
            pltpu.VMEM((3, face_rows, LANES), F32),
            *[pltpu.SemaphoreType.DMA((2, len(parcels), 3, n_sub))] * 3,
            *[pltpu.VMEM((2, 2, rows // fold, LANES), F32) for rows in rows_of],
            *[pltpu.VMEM((2, 3, n_sub, rows // fold, LANES), F32) for rows in rows_of],
        ],
        compiler_params=pltpu.CompilerParams(collective_id=0, has_side_effects=True),
    )(
        modal_state.transpose(1, 0, 2),
        star_mats.transpose(1, 2, 0, 3),
        face_flux.transpose(0, 2, 3, 1, 4),
        stiffness,
        stiff_vol,
        face_proj.transpose(2, 0, 1),
        face_lifting_matrix.transpose(1, 0, 2),
        orient_maps,
        neighbours,
        face_orient,
        send_slots,
        fast_count,
    )
    return out.transpose(1, 0, 2)


def solution(mesh):
    split_last = ("dom", "sub")
    placed = (
        P(None, None, split_last),
        P(None, None, None, split_last),
        P(None, None, None, None, split_last),
        P(),
        P(),
        P(),
        P(),
        P(),
        P(None, split_last),
        P(None, split_last),
        P(None, split_last),
        P(split_last),
    )
    return jax.shard_map(
        functools.partial(local, mesh.shape["dom"], mesh.shape["sub"]),
        mesh=mesh,
        in_specs=placed,
        out_specs=P(None, None, split_last),
        check_vma=False,
    )
```

```python
import functools

import jax
import jax.numpy as jnp
from jax import lax
from jax.experimental import pallas as pl
from jax.experimental.pallas import tpu as pltpu
from jax.sharding import PartitionSpec as P

DEGREE = 5
LANES = 128
F32 = jnp.float32
BF16 = jnp.bfloat16


def up(value, multiple):
    return -(-value // multiple) * multiple


def split(x):
    hi = x.astype(BF16)
    return hi, (x - hi.astype(F32)).astype(BF16)


def stacked(x):
    hi, lo = split(x)
    return jnp.concatenate([hi, lo], axis=0)


def dot(a, b):
    return jnp.dot(a, b, preferred_element_type=F32)


def rows3(x, depth):
    low = x - x.astype(BF16).astype(F32)
    rest = depth - 3 * x.shape[0]
    parts = [x, low, x]
    if rest:
        parts.append(jnp.zeros((rest, x.shape[1]), F32))
    return jnp.concatenate(parts, axis=0).astype(BF16)


def twice(x):
    return jnp.concatenate([x, x], axis=0)


def grow(x, rows):
    if rows == x.shape[0]:
        return x
    return jnp.concatenate([x, jnp.zeros((rows - x.shape[0], x.shape[1]), F32)], axis=0)


def row_of(ref, *lead_and_row):
    lead, row = lead_and_row[:-1], lead_and_row[-1]
    return ref[(*lead, pl.ds(row, 1), slice(None))]


def at_columns(rows, columns, test):
    row = lax.broadcasted_iota(jnp.int32, (rows, columns), 0)
    column = lax.broadcasted_iota(jnp.int32, (rows, columns), 1)
    return jnp.where(test(row, column), 1.0, 0.0).astype(BF16)


def shifted(rows, columns, shift):
    return at_columns(rows, columns, lambda row, column: column == row + shift)


def columns3(w, depth):
    hi, lo = split(w)
    inner = w.shape[1]
    first = at_columns(inner, depth, lambda r, c: (c == r) | (c == r + inner))
    return (dot(hi, first) + dot(lo, shifted(inner, depth, 2 * inner))).astype(BF16)


def kernel(
    sizes,
    state_hbm,
    star_hbm,
    flux_hbm,
    stiff_hbm,
    vol_hbm,
    proj_hbm,
    lift_hbm,
    maps_hbm,
    near_idx_ref,
    orient_ref,
    slots_ref,
    count_ref,
    out_ref,
    star_ref,
    flux_ref,
    stiff_ref,
    vol_ref,
    proj_ref,
    lift_ref,
    maps_ref,
    load_sem,
    star_pair,
    y_even,
    y_odd,
    pair_even,
    pair_odd,
    part,
    part_pair,
    taylor,
    slow,
    part_rows,
    trace,
    table,
    near,
    remote,
    pred_w,
    vol_w,
    proj_w,
    own_w,
    near_w,
    hot_local,
    hot_remote,
    hot_send,
    mask,
    send,
    recv,
    send_sem,
    recv_sem,
    forward_sem,
):
    n_dom, n_sub, modes, fields, face_pad, slots = sizes
    faces = 4
    face_modes = maps_ref.shape[1]
    half = LANES // 2
    pairs = (fields + 1) // 2
    depth = pred_w.shape[1]
    mode_pad = up(modes, 16)
    fold = LANES // slots
    table_rows = table.shape[0]
    fold_rows = table_rows // fold
    group = n_sub * slots
    face_rows = faces * face_pad
    own_count = faces * LANES
    loads = [
        pltpu.make_async_copy(source, target, load_sem.at[i])
        for i, (source, target) in enumerate(
            [
                (stiff_hbm, stiff_ref),
                (state_hbm, out_ref),
                (star_hbm, star_ref),
                (proj_hbm, proj_ref),
                (vol_hbm, vol_ref),
                (lift_hbm, lift_ref),
                (maps_hbm, maps_ref),
                (flux_hbm, flux_ref),
            ]
        )
    ]
    for load in loads:
        load.start()
    dom, sub = lax.axis_index("dom"), lax.axis_index("sub")
    has_low, has_high = dom > 0, dom < n_dom - 1

    barrier = pltpu.get_barrier_semaphore()

    def greet(d, s):
        pl.semaphore_signal(
            barrier, inc=1, device_id={"dom": d, "sub": s}, device_id_type=pl.DeviceIdType.MESH
        )

    chips = n_sub // 2
    chip, core = sub // 2, lax.rem(sub, 2)
    sibling = 2 * chip + 1 - core

    greet(dom, sibling)
    for k in range(1, chips):
        greet(dom, 2 * lax.rem(chip + k, chips) + core)

    @pl.when(has_low)
    def _():
        for c in range(chips):
            greet(dom - 1, 2 * c + core)

    @pl.when(has_high)
    def _():
        for c in range(chips):
            greet(dom + 1, 2 * c + core)

    @pl.when(jnp.logical_not(has_low))
    def _():
        recv[:, 1] = jnp.zeros((2, *recv.shape[2:]), F32)

    @pl.when(jnp.logical_not(has_high))
    def _():
        recv[:, 2] = jnp.zeros((2, *recv.shape[2:]), F32)

    def one_hot(row, rows):
        at = lax.broadcasted_iota(jnp.int32, (rows, LANES), 0)
        return jnp.where(at == row, 1.0, 0.0).astype(BF16)

    tiled = dot(
        stacked(grow(slots_ref[...].astype(F32), 8)),
        at_columns(slots, LANES, lambda row, column: column % slots == row),
    )
    tiled = (tiled[:8] + tiled[8:]).astype(jnp.int32)
    for i in range(2):
        hot_send[:, i * LANES : (i + 1) * LANES] = one_hot(tiled[i : i + 1, :], own_count)

    def by_direction(ref):
        rows = jnp.concatenate([ref[d] for d in range(3)], axis=0)
        return grow(rows, pred_w.shape[0])

    def by_face(ref):
        return jnp.concatenate([grow(ref[:, j, :], face_pad) for j in range(faces)], axis=0)

    loads[0].wait()
    pred_w[...] = columns3(-by_direction(stiff_ref), depth)

    chunks = [tuple(range(f, min(f + 2, fields))) for f in range(0, fields, 2)]
    pair_chunks = [tuple(range(i, min(i + 2, pairs))) for i in range(0, pairs, 2)]

    def cols(chunk):
        return slice(chunk[0] * LANES, (chunk[-1] + 1) * LANES)

    def lane(i):
        return slice(i * LANES, (i + 1) * LANES)

    def side_by_side(values):
        return values[0] if len(values) == 1 else jnp.concatenate(values, axis=1)

    def stiff_rows(value):
        return dot(pred_w[...], rows3(value, depth))[: 3 * modes]

    blocks = [(start, min(16, modes - start)) for start in range(0, modes, 16)]

    def contract(source, terms, rows, targets):
        values = [[] for _ in targets]
        for start, count in blocks:
            totals = [[None] * 3 for _ in targets]
            for g in range(terms):
                for d in range(3):
                    first = d * modes + start
                    item = source[first : first + count, lane(g)]
                    for i, f in enumerate(targets):
                        term = row_of(rows, f, g, d) * item
                        total = totals[i][d]
                        totals[i][d] = term if total is None else total + term
            for i, total in enumerate(totals):
                values[i].append(total[0] + total[1] + total[2])
        return [jnp.concatenate(value, axis=0) for value in values]

    low_half = lax.broadcasted_iota(jnp.int32, (modes, LANES), 1) < half

    def pair_up(first, second):
        return jnp.where(low_half, first, pltpu.roll(second, half, 1))

    def contract_pairs(source, chunk):
        targets = [f for i in chunk for f in (2 * i, 2 * i + 1) if f < fields]
        values = contract(source, pairs, star_pair, targets)
        if len(targets) < 2 * len(chunk):
            values.append(jnp.zeros((modes, LANES), F32))
        result = []
        for i in range(len(chunk)):
            even, odd = values[2 * i], values[2 * i + 1]
            result.append(
                jnp.where(low_half, even, odd)
                + pltpu.roll(jnp.where(low_half, odd, even), half, 1)
            )
        return side_by_side(result)

    def project(chunk, value):
        rows = rows3(value, depth)
        part_rows[:, cols(chunk)] = rows
        value = dot(proj_w[...], rows)
        for i, g in enumerate(chunk):
            for j in range(faces):
                trace[j, g * face_modes : g * face_modes + face_pad, :] = value[
                    j * face_pad : (j + 1) * face_pad, lane(i)
                ]

    def flux_rows(side, src, chunk):
        found = [[] for _ in chunk]
        for j in range(faces):
            totals = [None] * len(chunk)
            for g in range(fields):
                item = src[j, g * face_modes : g * face_modes + face_pad, :]
                for i, f in enumerate(chunk):
                    term = row_of(flux_ref, side, f, g, j) * item
                    totals[i] = term if totals[i] is None else totals[i] + term
            for i, total in enumerate(totals):
                found[i].append(total)
        return [jnp.concatenate(value, axis=0) for value in found]

    def add_out(chunk, value):
        for i, f in enumerate(chunk):
            out_ref[f] = out_ref[f] + value[:modes, lane(i)]

    def out_copy(ex, which, target, region, at):
        return pltpu.make_async_remote_copy(
            src_ref=send.at[ex, which],
            dst_ref=recv.at[ex, region, sub],
            send_sem=send_sem.at[ex, region, at],
            recv_sem=recv_sem.at[ex, region, sub],
            device_id=target,
            device_id_type=pl.DeviceIdType.MESH,
        )

    def exchange_copies(ex):
        inner = [out_copy(ex, 0, {"dom": dom, "sub": sibling}, 0, 0)]
        for k in range(1, chips):
            target = {"dom": dom, "sub": 2 * lax.rem(chip + k, chips) + core}
            inner.append(out_copy(ex, 0, target, 0, k))
        lower = [
            out_copy(ex, 1, {"dom": dom - 1, "sub": 2 * c + core}, 2, c) for c in range(chips)
        ]
        upper = [
            out_copy(ex, 1, {"dom": dom + 1, "sub": 2 * c + core}, 1, c) for c in range(chips)
        ]
        return inner, lower, upper

    def arrival(ex, region, s):
        return pltpu.make_async_remote_copy(
            src_ref=send.at[ex, 0],
            dst_ref=recv.at[ex, region, s],
            send_sem=send_sem.at[ex, region, 0],
            recv_sem=recv_sem.at[ex, region, s],
            device_id={"dom": dom, "sub": sub},
            device_id_type=pl.DeviceIdType.MESH,
        )

    def forward(ex, region, s):
        return pltpu.make_async_remote_copy(
            src_ref=recv.at[ex, region, s],
            dst_ref=recv.at[ex, region, s],
            send_sem=forward_sem.at[ex, region, s],
            recv_sem=recv_sem.at[ex, region, s],
            device_id={"dom": dom, "sub": sibling},
            device_id_type=pl.DeviceIdType.MESH,
        )

    def each_region(do, side):
        @pl.when(has_low)
        def _():
            for c in range(chips):
                do(1, 2 * c + side)

        @pl.when(has_high)
        def _():
            for c in range(chips):
                do(2, 2 * c + side)

        for k in range(1, chips):
            do(0, 2 * lax.rem(chip + k, chips) + side)

    section = lax.broadcasted_iota(jnp.int32, (fold_rows, LANES), 1) // slots

    def send_traces(ex):
        for j in range(faces):
            hi, lo = split(trace[j])
            table[:, lane(j)] = hi
            table[:, lane(faces + j)] = lo
        picked = dot(table[...], twice(hot_send[...]))
        for i in range(2):
            packed = picked[:fold_rows, lane(i)]
            for a in range(1, fold):
                packed = jnp.where(
                    section == a, picked[a * fold_rows : (a + 1) * fold_rows, lane(i)], packed
                )
            send[ex, i] = packed
            if i == 0:
                recv[ex, 0, sub] = packed
        if ex == 0:
            pl.semaphore_wait(
                barrier, chips * (1 + has_low.astype(jnp.int32) + has_high.astype(jnp.int32))
            )
        inner, lower, upper = exchange_copies(ex)

        @pl.when(has_low)
        def _():
            for copy in lower:
                copy.start()

        @pl.when(has_high)
        def _():
            for copy in upper:
                copy.start()

        for copy in inner:
            copy.start()

    def own_update():
        for jj in range(0, faces, 2):
            at = slice(jj * LANES, (jj + 2) * LANES)
            found = dot(table[...], twice(hot_local[:, at]))
            near[jj] = found[:, :LANES]
            near[jj + 1] = found[:, LANES:]
        for chunk in chunks:
            y_even[:, cols(chunk)] = dot(vol_w[...], part_rows[:, cols(chunk)])[: 3 * modes]
        for chunk in chunks:
            volume = side_by_side(contract(y_even, fields, star_ref, chunk))
            own = side_by_side(flux_rows(0, trace, chunk))
            add_out(chunk, volume + dot(own_w[...], rows3(own, 3 * face_rows))[:modes])

    def take_arrivals(ex):
        def pass_on(region, s):
            arrival(ex, region, s).wait_recv()
            forward(ex, region, s).start()

        each_region(pass_on, core)
        arrival(ex, 0, sibling).wait_recv()
        each_region(lambda region, s: arrival(ex, region, s).wait_recv(), 1 - core)

        for region in range(3):
            for b in range(n_sub // fold):
                parts = [recv[ex, region, b * fold + i] for i in range(fold)]
                for a in range(fold):
                    value = None
                    for i in range(fold):
                        moved = parts[i]
                        if i != a:
                            moved = pltpu.roll(moved, ((i - a) * slots) % LANES, 1)
                        value = moved if value is None else jnp.where(section == i, moved, value)
                    first = region * group + b * LANES
                    rows = slice(a * fold_rows, (a + 1) * fold_rows)
                    hi, lo = split(value)
                    remote[rows, first : first + LANES] = hi
                    first = first + 3 * group
                    remote[rows, first : first + LANES] = lo

    def near_update():
        for jj in range(0, faces, 2):
            at = slice(jj * LANES, (jj + 2) * LANES)
            found = dot(remote[...], twice(hot_remote[:, at]))
            near[jj] = near[jj] + found[:, :LANES]
            near[jj + 1] = near[jj + 1] + found[:, LANES:]
        masks = [mask[o].astype(BF16) for o in range(3)]
        for chunk in chunks:
            pieces = []
            for value in flux_rows(1, near, chunk):
                hi, lo = split(value)
                hi = [hi * masks[o] for o in range(3)]
                lo = [lo * masks[o] for o in range(3)]
                pieces.append(jnp.concatenate(hi + lo + hi, axis=0))
            add_out(chunk, dot(near_w[...], side_by_side(pieces)))

    def finish_sends(ex):
        inner, lower, upper = exchange_copies(ex)
        for copy in inner:
            copy.wait_send()

        @pl.when(has_low)
        def _():
            for copy in lower:
                copy.wait_send()

        @pl.when(has_high)
        def _():
            for copy in upper:
                copy.wait_send()

        each_region(lambda region, s: forward(ex, region, s).wait_send(), core)

    def prepare_update():
        for j in range(faces):
            row = near_idx_ref[j : j + 1, :]
            hot_local[:, lane(j)] = one_hot(row, own_count)
            hot_remote[:, lane(j)] = one_hot(row - own_count, 3 * group)
            turn = orient_ref[j : j + 1, :]
            for o in range(3):
                mask[o, j * face_pad : (j + 1) * face_pad, :] = jnp.broadcast_to(
                    jnp.where(turn == o, 1.0, 0.0), (face_pad, LANES)
                )
        vol_w[...] = columns3(by_direction(vol_ref), depth)
        same = shifted(mode_pad, modes, 0)
        lift = []
        for value in split(-by_face(lift_ref)):
            lift.append(
                lax.dot_general(same, value, (((1,), (1,)), ((), ())), preferred_element_type=F32)
            )
        hi, lo = lift[0].astype(BF16), lift[1].astype(BF16)
        own_w[:, :face_rows] = hi
        own_w[:, face_rows : 2 * face_rows] = hi
        own_w[:, 2 * face_rows :] = lo
        turned = None
        map_pad = up(face_pad, 16)
        for o in range(3):
            place = at_columns(
                face_modes,
                3 * face_rows,
                lambda row, column: (column // face_rows == o) & (column % face_pad == row),
            )
            both = dot(stacked(grow(maps_ref[o], map_pad)), place)
            term = both[:face_pad] + both[map_pad : map_pad + face_pad]
            turned = term if turned is None else turned + term
        turned = jnp.concatenate([turned] * faces, axis=0)
        row = lax.broadcasted_iota(jnp.int32, turned.shape, 0)
        column = lax.broadcasted_iota(jnp.int32, turned.shape, 1)
        turned = jnp.where(column % face_rows // face_pad == row // face_pad, turned, 0.0)
        turned_hi, turned_lo = split(turned)
        value = dot(hi, turned_hi) + dot(lo, turned_hi) + dot(hi, turned_lo)
        hi, lo = split(value)
        near_w[:, : 3 * face_rows] = hi
        near_w[:, 3 * face_rows : 6 * face_rows] = hi
        near_w[:, 6 * face_rows :] = lo

    def prepare_pairs():
        low = lax.broadcasted_iota(jnp.int32, (8, LANES), 1) < half
        for f in range(fields):
            for i in range(pairs):
                first = grow(star_ref[f, 2 * i], 8)
                if 2 * i + 1 < fields:
                    second = pltpu.roll(grow(star_ref[f, 2 * i + 1], 8), half, 1)
                else:
                    second = jnp.zeros((8, LANES), F32)
                star_pair[f, i] = jnp.where(low, first, second)[:3]

    def sum_slow():
        for f in range(fields):
            total = part[:, lane(f)]
            weight = 1.0
            for k in range(DEGREE):
                weight = weight / (k + 2)
                total = total + ((2.0 ** (k + 2) - 2.0) * weight) * taylor[k, :, lane(f)]
            slow[:, lane(f)] = total

    loads[1].wait()
    for chunk in chunks:
        value = side_by_side([out_ref[f] for f in chunk])
        part[:, cols(chunk)] = value
        y_even[:, cols(chunk)] = stiff_rows(value)
    loads[2].wait()

    weight = 1.0
    source, target = y_even, y_odd
    for k in range(DEGREE - 1):
        weight = weight / (k + 2)
        for chunk in chunks:
            value = side_by_side(contract(source, fields, star_ref, chunk))
            taylor[k, :, cols(chunk)] = value
            part[:, cols(chunk)] = part[:, cols(chunk)] + weight * value
            target[:, cols(chunk)] = stiff_rows(value)
        source, target = target, source
    weight = weight / (DEGREE + 1)
    loads[3].wait()
    proj_w[...] = columns3(by_face(proj_ref), depth)
    for chunk in chunks:
        value = side_by_side(contract(source, fields, star_ref, chunk))
        taylor[DEGREE - 1, :, cols(chunk)] = value
        value = part[:, cols(chunk)] + weight * value
        part[:, cols(chunk)] = value
        project(chunk, value)
    send_traces(0)

    for load in loads[4:]:
        load.wait()
    prepare_update()
    own_update()
    prepare_pairs()
    sum_slow()
    take_arrivals(0)
    near_update()
    finish_sends(0)

    for chunk in pair_chunks:
        value = []
        for i in chunk:
            first = out_ref[2 * i]
            second = out_ref[min(2 * i + 1, fields - 1)]
            value.append(pair_up(first, second))
        value = side_by_side(value)
        part_pair[:, cols(chunk)] = value
        pair_even[:, cols(chunk)] = stiff_rows(value)

    weight = 1.0
    source, target = pair_even, pair_odd
    for k in range(DEGREE - 1):
        weight = weight / (k + 2)
        for chunk in pair_chunks:
            value = contract_pairs(source, chunk)
            part_pair[:, cols(chunk)] = part_pair[:, cols(chunk)] + weight * value
            target[:, cols(chunk)] = stiff_rows(value)
        source, target = target, source
    weight = weight / (DEGREE + 1)
    is_fast = lax.broadcasted_iota(jnp.int32, (modes, LANES), 1) < count_ref[0]
    for chunk in pair_chunks:
        value = part_pair[:, cols(chunk)] + weight * contract_pairs(source, chunk)
        for n, i in enumerate(chunk):
            item = value[:, lane(n)]
            both = [item, pltpu.roll(item, half, 1)]
            mine = tuple(f for f in (2 * i, 2 * i + 1) if f < fields)
            mixed = [
                jnp.where(is_fast, both[q], slow[:, lane(f)]) for q, f in enumerate(mine)
            ]
            project(mine, side_by_side(mixed))
    send_traces(1)
    own_update()
    take_arrivals(1)
    near_update()
    finish_sends(1)


def local(
    n_dom,
    n_sub,
    modal_state,
    star_mats,
    face_flux,
    stiffness,
    stiff_vol,
    face_proj,
    face_lifting_matrix,
    orient_maps,
    neighbours,
    face_orient,
    send_slots,
    fast_count,
):
    modes, fields, elems = modal_state.shape
    face_modes = orient_maps.shape[1]
    slots = send_slots.shape[1]
    fold = LANES // slots
    face_pad, mode_pad = up(face_modes, 8), up(modes, 16)
    table_rows = up((fields - 1) * face_modes + face_pad, 8 * fold)
    group = n_sub * slots
    width = fields * elems
    pairs = (fields + 1) // 2
    depth, rows3 = up(3 * modes, 16), up(3 * modes, 16)
    face_rows = 4 * face_pad
    any_space = pl.BlockSpec(memory_space=pl.ANY)
    vmem = pl.BlockSpec(memory_space=pltpu.VMEM)
    out = pl.pallas_call(
        functools.partial(kernel, (n_dom, n_sub, modes, fields, face_pad, slots)),
        out_shape=pltpu.VMEM((fields, modes, elems), F32),
        in_specs=[any_space] * 8 + [vmem] * 3 + [pl.BlockSpec(memory_space=pltpu.SMEM)],
        out_specs=vmem,
        scratch_shapes=[
            pltpu.VMEM((fields, fields, 3, elems), F32),
            pltpu.VMEM((2, fields, fields, 4, elems), F32),
            pltpu.VMEM((3, modes, modes), F32),
            pltpu.VMEM((3, modes, modes), F32),
            pltpu.VMEM((face_modes, 4, modes), F32),
            pltpu.VMEM((face_modes, 4, modes), F32),
            pltpu.VMEM((3, face_modes, face_modes), F32),
            pltpu.SemaphoreType.DMA((8,)),
            pltpu.VMEM((fields, pairs, 3, elems), F32),
            pltpu.VMEM((3 * modes, width), F32),
            pltpu.VMEM((3 * modes, width), F32),
            pltpu.VMEM((3 * modes, pairs * elems), F32),
            pltpu.VMEM((3 * modes, pairs * elems), F32),
            pltpu.VMEM((modes, width), F32),
            pltpu.VMEM((modes, pairs * elems), F32),
            pltpu.VMEM((DEGREE, modes, width), F32),
            pltpu.VMEM((modes, width), F32),
            pltpu.VMEM((depth, width), BF16),
            pltpu.VMEM((4, table_rows, elems), F32),
            pltpu.VMEM((table_rows, 8 * elems), BF16),
            pltpu.VMEM((4, table_rows, elems), F32),
            pltpu.VMEM((table_rows, 6 * group), BF16),
            pltpu.VMEM((rows3, depth), BF16),
            pltpu.VMEM((rows3, depth), BF16),
            pltpu.VMEM((face_rows, depth), BF16),
            pltpu.VMEM((mode_pad, 3 * face_rows), BF16),
            pltpu.VMEM((mode_pad, 9 * face_rows), BF16),
            pltpu.VMEM((4 * elems, 4 * elems), BF16),
            pltpu.VMEM((3 * group, 4 * elems), BF16),
            pltpu.VMEM((4 * elems, 2 * LANES), BF16),
            pltpu.VMEM((3, face_rows, LANES), F32),
            pltpu.VMEM((2, 2, table_rows // fold, LANES), F32),
            pltpu.VMEM((2, 3, n_sub, table_rows // fold, LANES), F32),
            pltpu.SemaphoreType.DMA((2, 3, n_sub)),
            pltpu.SemaphoreType.DMA((2, 3, n_sub)),
            pltpu.SemaphoreType.DMA((2, 3, n_sub)),
        ],
        compiler_params=pltpu.CompilerParams(collective_id=0, has_side_effects=True),
    )(
        modal_state.transpose(1, 0, 2),
        star_mats.transpose(1, 2, 0, 3),
        face_flux.transpose(0, 2, 3, 1, 4),
        stiffness,
        stiff_vol,
        face_proj.transpose(2, 0, 1),
        face_lifting_matrix.transpose(1, 0, 2),
        orient_maps,
        neighbours,
        face_orient,
        send_slots,
        fast_count,
    )
    return out.transpose(1, 0, 2)


def solution(mesh):
    split_last = ("dom", "sub")
    placed = (
        P(None, None, split_last),
        P(None, None, None, split_last),
        P(None, None, None, None, split_last),
        P(),
        P(),
        P(),
        P(),
        P(),
        P(None, split_last),
        P(None, split_last),
        P(None, split_last),
        P(split_last),
    )
    return jax.shard_map(
        functools.partial(local, mesh.shape["dom"], mesh.shape["sub"]),
        mesh=mesh,
        in_specs=placed,
        out_specs=P(None, None, split_last),
        check_vma=False,
    )
```

```python
import functools

import jax
import jax.numpy as jnp
from jax import lax
from jax.experimental import pallas as pl
from jax.experimental.pallas import tpu as pltpu
from jax.sharding import PartitionSpec as P

DEGREE = 5
LANES = 128
F32 = jnp.float32
BF16 = jnp.bfloat16


def up(value, multiple):
    return -(-value // multiple) * multiple


def split(x):
    hi = x.astype(BF16)
    return hi, (x - hi.astype(F32)).astype(BF16)


def stacked(x):
    hi, lo = split(x)
    return jnp.concatenate([hi, lo], axis=0)


def dot(a, b):
    return jnp.dot(a, b, preferred_element_type=F32)


def rows3(x, depth):
    low = x - x.astype(BF16).astype(F32)
    rest = depth - 3 * x.shape[0]
    parts = [x, low, x]
    if rest:
        parts.append(jnp.zeros((rest, x.shape[1]), F32))
    return jnp.concatenate(parts, axis=0).astype(BF16)


def twice(x):
    return jnp.concatenate([x, x], axis=0)


def grow(x, rows):
    if rows == x.shape[0]:
        return x
    return jnp.concatenate([x, jnp.zeros((rows - x.shape[0], x.shape[1]), F32)], axis=0)


def row_of(ref, *lead_and_row):
    lead, row = lead_and_row[:-1], lead_and_row[-1]
    return ref[(*lead, pl.ds(row, 1), slice(None))]


def at_columns(rows, columns, test):
    row = lax.broadcasted_iota(jnp.int32, (rows, columns), 0)
    column = lax.broadcasted_iota(jnp.int32, (rows, columns), 1)
    return jnp.where(test(row, column), 1.0, 0.0).astype(BF16)


def shifted(rows, columns, shift):
    return at_columns(rows, columns, lambda row, column: column == row + shift)


def columns3(w, depth):
    hi, lo = split(w)
    inner = w.shape[1]
    first = at_columns(inner, depth, lambda r, c: (c == r) | (c == r + inner))
    return (dot(hi, first) + dot(lo, shifted(inner, depth, 2 * inner))).astype(BF16)


def kernel(
    sizes,
    state_hbm,
    star_hbm,
    flux_hbm,
    stiff_hbm,
    vol_hbm,
    proj_hbm,
    lift_hbm,
    maps_hbm,
    near_idx_hbm,
    orient_hbm,
    slots_hbm,
    count_ref,
    out_ref,
    near_idx_ref,
    orient_ref,
    slots_ref,
    star_ref,
    flux_ref,
    stiff_ref,
    vol_ref,
    proj_ref,
    lift_ref,
    maps_ref,
    load_sem,
    star_pair,
    y_even,
    y_odd,
    pair_even,
    pair_odd,
    part,
    part_pair,
    taylor,
    slow,
    part_rows,
    trace,
    table,
    near,
    remote,
    pred_w,
    vol_w,
    proj_w,
    own_w,
    near_w,
    hot_local,
    hot_remote,
    hot_send,
    mask,
    send,
    recv,
    send_sem,
    recv_sem,
    forward_sem,
):
    n_dom, n_sub, modes, fields, face_pad, slots = sizes
    faces = 4
    face_modes = maps_ref.shape[1]
    half = LANES // 2
    pairs = (fields + 1) // 2
    depth = pred_w.shape[1]
    mode_pad = up(modes, 16)
    fold = LANES // slots
    table_rows = table.shape[0]
    fold_rows = table_rows // fold
    group = n_sub * slots
    face_rows = faces * face_pad
    own_count = faces * LANES
    loads = [
        pltpu.make_async_copy(source, target, load_sem.at[i])
        for i, (source, target) in enumerate(
            [
                (slots_hbm, slots_ref),
                (stiff_hbm, stiff_ref),
                (state_hbm, out_ref),
                (star_hbm, star_ref),
                (proj_hbm, proj_ref),
                (vol_hbm, vol_ref),
                (lift_hbm, lift_ref),
                (maps_hbm, maps_ref),
                (flux_hbm, flux_ref),
                (near_idx_hbm, near_idx_ref),
                (orient_hbm, orient_ref),
            ]
        )
    ]
    for load in loads:
        load.start()
    dom, sub = lax.axis_index("dom"), lax.axis_index("sub")
    has_low, has_high = dom > 0, dom < n_dom - 1

    barrier = pltpu.get_barrier_semaphore()

    def greet(d, s):
        pl.semaphore_signal(
            barrier, inc=1, device_id={"dom": d, "sub": s}, device_id_type=pl.DeviceIdType.MESH
        )

    chips = n_sub // 2
    chip, core = sub // 2, lax.rem(sub, 2)
    sibling = 2 * chip + 1 - core

    greet(dom, sibling)
    for k in range(1, chips):
        greet(dom, 2 * lax.rem(chip + k, chips) + core)

    @pl.when(has_low)
    def _():
        for c in range(chips):
            greet(dom - 1, 2 * c + core)

    @pl.when(has_high)
    def _():
        for c in range(chips):
            greet(dom + 1, 2 * c + core)

    @pl.when(jnp.logical_not(has_low))
    def _():
        recv[:, 1] = jnp.zeros((2, *recv.shape[2:]), F32)

    @pl.when(jnp.logical_not(has_high))
    def _():
        recv[:, 2] = jnp.zeros((2, *recv.shape[2:]), F32)

    def one_hot(row, rows):
        at = lax.broadcasted_iota(jnp.int32, (rows, LANES), 0)
        return jnp.where(at == row, 1.0, 0.0).astype(BF16)

    loads[0].wait()
    tiled = dot(
        stacked(grow(slots_ref[...].astype(F32), 8)),
        at_columns(slots, LANES, lambda row, column: column % slots == row),
    )
    tiled = (tiled[:8] + tiled[8:]).astype(jnp.int32)
    for i in range(2):
        hot_send[:, i * LANES : (i + 1) * LANES] = one_hot(tiled[i : i + 1, :], own_count)

    def by_direction(ref):
        rows = jnp.concatenate([ref[d] for d in range(3)], axis=0)
        return grow(rows, pred_w.shape[0])

    def by_face(ref):
        return jnp.concatenate([grow(ref[:, j, :], face_pad) for j in range(faces)], axis=0)

    loads[1].wait()
    pred_w[...] = columns3(-by_direction(stiff_ref), depth)

    chunks = [tuple(range(f, min(f + 2, fields))) for f in range(0, fields, 2)]
    pair_chunks = [tuple(range(i, min(i + 2, pairs))) for i in range(0, pairs, 2)]

    def cols(chunk):
        return slice(chunk[0] * LANES, (chunk[-1] + 1) * LANES)

    def lane(i):
        return slice(i * LANES, (i + 1) * LANES)

    def side_by_side(values):
        return values[0] if len(values) == 1 else jnp.concatenate(values, axis=1)

    def stiff_rows(value):
        return dot(pred_w[...], rows3(value, depth))[: 3 * modes]

    blocks = [(start, min(16, modes - start)) for start in range(0, modes, 16)]

    def contract(source, terms, rows, targets):
        values = [[] for _ in targets]
        for start, count in blocks:
            totals = [[None] * 3 for _ in targets]
            for g in range(terms):
                for d in range(3):
                    first = d * modes + start
                    item = source[first : first + count, lane(g)]
                    for i, f in enumerate(targets):
                        term = row_of(rows, f, g, d) * item
                        total = totals[i][d]
                        totals[i][d] = term if total is None else total + term
            for i, total in enumerate(totals):
                values[i].append(total[0] + total[1] + total[2])
        return [jnp.concatenate(value, axis=0) for value in values]

    low_half = lax.broadcasted_iota(jnp.int32, (modes, LANES), 1) < half

    def pair_up(first, second):
        return jnp.where(low_half, first, pltpu.roll(second, half, 1))

    def contract_pairs(source, chunk):
        targets = [f for i in chunk for f in (2 * i, 2 * i + 1) if f < fields]
        values = contract(source, pairs, star_pair, targets)
        if len(targets) < 2 * len(chunk):
            values.append(jnp.zeros((modes, LANES), F32))
        result = []
        for i in range(len(chunk)):
            even, odd = values[2 * i], values[2 * i + 1]
            result.append(
                jnp.where(low_half, even, odd)
                + pltpu.roll(jnp.where(low_half, odd, even), half, 1)
            )
        return side_by_side(result)

    def project(chunk, value):
        rows = rows3(value, depth)
        part_rows[:, cols(chunk)] = rows
        value = dot(proj_w[...], rows)
        for i, g in enumerate(chunk):
            for j in range(faces):
                trace[j, g * face_modes : g * face_modes + face_pad, :] = value[
                    j * face_pad : (j + 1) * face_pad, lane(i)
                ]

    def flux_rows(side, src, chunk, of=range(faces)):
        found = [[] for _ in chunk]
        for j in of:
            totals = [None] * len(chunk)
            for g in range(fields):
                item = src[j, g * face_modes : g * face_modes + face_pad, :]
                for i, f in enumerate(chunk):
                    term = row_of(flux_ref, side, f, g, j) * item
                    totals[i] = term if totals[i] is None else totals[i] + term
            for i, total in enumerate(totals):
                found[i].append(total)
        return [jnp.concatenate(value, axis=0) for value in found]

    def add_out(chunk, value):
        for i, f in enumerate(chunk):
            out_ref[f] = out_ref[f] + value[:modes, lane(i)]

    def out_copy(ex, which, target, region, at):
        return pltpu.make_async_remote_copy(
            src_ref=send.at[ex, which],
            dst_ref=recv.at[ex, region, sub],
            send_sem=send_sem.at[ex, region, at],
            recv_sem=recv_sem.at[ex, region, sub],
            device_id=target,
            device_id_type=pl.DeviceIdType.MESH,
        )

    def exchange_copies(ex):
        inner = [out_copy(ex, 0, {"dom": dom, "sub": sibling}, 0, 0)]
        for k in range(1, chips):
            target = {"dom": dom, "sub": 2 * lax.rem(chip + k, chips) + core}
            inner.append(out_copy(ex, 0, target, 0, k))
        lower, upper = [], []
        for k in reversed(range(chips)):
            at = 2 * lax.rem(chip + k, chips) + core
            lower.append(out_copy(ex, 1, {"dom": dom - 1, "sub": at}, 2, k))
            upper.append(out_copy(ex, 1, {"dom": dom + 1, "sub": at}, 1, k))
        return inner, lower, upper

    def arrival(ex, region, s):
        return pltpu.make_async_remote_copy(
            src_ref=send.at[ex, 0],
            dst_ref=recv.at[ex, region, s],
            send_sem=send_sem.at[ex, region, 0],
            recv_sem=recv_sem.at[ex, region, s],
            device_id={"dom": dom, "sub": sub},
            device_id_type=pl.DeviceIdType.MESH,
        )

    def forward(ex, region, s):
        return pltpu.make_async_remote_copy(
            src_ref=recv.at[ex, region, s],
            dst_ref=recv.at[ex, region, s],
            send_sem=forward_sem.at[ex, region, s],
            recv_sem=recv_sem.at[ex, region, s],
            device_id={"dom": dom, "sub": sibling},
            device_id_type=pl.DeviceIdType.MESH,
        )

    def each_region(do, side):
        for k in range(1, chips):
            do(0, 2 * lax.rem(chip + k, chips) + side)
        for k in range(chips):
            at = 2 * lax.rem(chip + k, chips) + side

            @pl.when(has_low)
            def _():
                do(1, at)

            @pl.when(has_high)
            def _():
                do(2, at)

    section = lax.broadcasted_iota(jnp.int32, (fold_rows, LANES), 1) // slots

    def send_traces(ex):
        picked = []
        for a in range(0, fold, 2):
            rows = slice(a * fold_rows, (a + 2) * fold_rows)
            for j in range(faces):
                hi, lo = split(trace[j, rows, :])
                table[rows, lane(j)] = hi
                table[rows, lane(faces + j)] = lo
            found = dot(table[rows, :], twice(hot_send[...]))
            picked += [found[:fold_rows], found[fold_rows:]]
        for i in range(2):
            packed = picked[0][:, lane(i)]
            for a in range(1, fold):
                packed = jnp.where(section == a, picked[a][:, lane(i)], packed)
            send[ex, i] = packed
            if i == 0:
                recv[ex, 0, sub] = packed
        if ex == 0:
            pl.semaphore_wait(
                barrier, chips * (1 + has_low.astype(jnp.int32) + has_high.astype(jnp.int32))
            )
        inner, lower, upper = exchange_copies(ex)

        @pl.when(has_low)
        def _():
            for copy in lower:
                copy.start()

        @pl.when(has_high)
        def _():
            for copy in upper:
                copy.start()

        for copy in inner:
            copy.start()

    def own_update():
        for jj in range(0, faces, 2):
            at = slice(jj * LANES, (jj + 2) * LANES)
            found = dot(table[...], twice(hot_local[:, at]))
            near[jj] = found[:, :LANES]
            near[jj + 1] = found[:, LANES:]
        for chunk in chunks:
            y_even[:, cols(chunk)] = dot(vol_w[...], part_rows[:, cols(chunk)])[: 3 * modes]
        for chunk in chunks:
            volume = side_by_side(contract(y_even, fields, star_ref, chunk))
            own = side_by_side(flux_rows(0, trace, chunk))
            add_out(chunk, volume + dot(own_w[...], rows3(own, 3 * face_rows))[:modes])

    def take_arrivals(ex):
        def pass_on(region, s):
            arrival(ex, region, s).wait_recv()
            forward(ex, region, s).start()

        each_region(pass_on, core)
        arrival(ex, 0, sibling).wait_recv()
        each_region(lambda region, s: arrival(ex, region, s).wait_recv(), 1 - core)

        for region in range(3):
            for b in range(n_sub // fold):
                parts = [recv[ex, region, b * fold + i] for i in range(fold)]
                for a in range(fold):
                    value = None
                    for i in range(fold):
                        moved = parts[i]
                        if i != a:
                            moved = pltpu.roll(moved, ((i - a) * slots) % LANES, 1)
                        value = moved if value is None else jnp.where(section == i, moved, value)
                    first = region * group + b * LANES
                    rows = slice(a * fold_rows, (a + 1) * fold_rows)
                    hi, lo = split(value)
                    remote[rows, first : first + LANES] = hi
                    first = first + 3 * group
                    remote[rows, first : first + LANES] = lo

    def near_update():
        for jj in range(0, faces, 2):
            at = slice(jj * LANES, (jj + 2) * LANES)
            found = dot(remote[...], twice(hot_remote[:, at]))
            near[jj] = near[jj] + found[:, :LANES]
            near[jj + 1] = near[jj + 1] + found[:, LANES:]
        for jj in range(0, faces, 2):
            rows = slice(jj * face_pad, (jj + 2) * face_pad)
            masks = [mask[o, rows, :].astype(BF16) for o in range(3)]
            for chunk in chunks:
                pieces = []
                for value in flux_rows(1, near, chunk, (jj, jj + 1)):
                    hi, lo = split(value)
                    hi = [hi * masks[o] for o in range(3)]
                    lo = [lo * masks[o] for o in range(3)]
                    pieces.append(jnp.concatenate(hi + lo + hi, axis=0))
                add_out(chunk, dot(near_w[jj // 2], side_by_side(pieces)))

    def finish_sends(ex):
        inner, lower, upper = exchange_copies(ex)
        for copy in inner:
            copy.wait_send()

        @pl.when(has_low)
        def _():
            for copy in lower:
                copy.wait_send()

        @pl.when(has_high)
        def _():
            for copy in upper:
                copy.wait_send()

        each_region(lambda region, s: forward(ex, region, s).wait_send(), core)

    def prepare_update():
        for j in range(faces):
            row = near_idx_ref[j : j + 1, :]
            hot_local[:, lane(j)] = one_hot(row, own_count)
            hot_remote[:, lane(j)] = one_hot(row - own_count, 3 * group)
            turn = orient_ref[j : j + 1, :]
            for o in range(3):
                mask[o, j * face_pad : (j + 1) * face_pad, :] = jnp.broadcast_to(
                    jnp.where(turn == o, 1.0, 0.0), (face_pad, LANES)
                )
        vol_w[...] = columns3(by_direction(vol_ref), depth)
        same = shifted(mode_pad, modes, 0)
        lift = []
        for value in split(-by_face(lift_ref)):
            lift.append(
                lax.dot_general(same, value, (((1,), (1,)), ((), ())), preferred_element_type=F32)
            )
        hi, lo = lift[0].astype(BF16), lift[1].astype(BF16)
        own_w[:, :face_rows] = hi
        own_w[:, face_rows : 2 * face_rows] = hi
        own_w[:, 2 * face_rows :] = lo
        map_pad = up(face_pad, 16)
        pair_rows = 2 * face_pad
        maps = [stacked(grow(maps_ref[o], map_pad)) for o in range(3)]
        for jj in range(0, faces, 2):
            turned = None
            for o in range(3):
                place = at_columns(
                    face_modes,
                    3 * pair_rows,
                    lambda row, column: (column // pair_rows == o) & (column % face_pad == row),
                )
                both = dot(maps[o], place)
                term = both[:face_pad] + both[map_pad : map_pad + face_pad]
                turned = term if turned is None else turned + term
            turned = jnp.concatenate([turned] * faces, axis=0)
            row = lax.broadcasted_iota(jnp.int32, turned.shape, 0)
            column = lax.broadcasted_iota(jnp.int32, turned.shape, 1)
            same_face = column % pair_rows // face_pad + jj == row // face_pad
            turned_hi, turned_lo = split(jnp.where(same_face, turned, 0.0))
            value = dot(hi, turned_hi) + dot(lo, turned_hi) + dot(hi, turned_lo)
            value_hi, value_lo = split(value)
            near_w[jj // 2, :, : 3 * pair_rows] = value_hi
            near_w[jj // 2, :, 3 * pair_rows : 6 * pair_rows] = value_hi
            near_w[jj // 2, :, 6 * pair_rows :] = value_lo

    def prepare_pairs():
        low = lax.broadcasted_iota(jnp.int32, (8, LANES), 1) < half
        for f in range(fields):
            for i in range(pairs):
                first = grow(star_ref[f, 2 * i], 8)
                if 2 * i + 1 < fields:
                    second = pltpu.roll(grow(star_ref[f, 2 * i + 1], 8), half, 1)
                else:
                    second = jnp.zeros((8, LANES), F32)
                star_pair[f, i] = jnp.where(low, first, second)[:3]

    def sum_slow():
        for f in range(fields):
            total = part[:, lane(f)]
            weight = 1.0
            for k in range(DEGREE):
                weight = weight / (k + 2)
                total = total + ((2.0 ** (k + 2) - 2.0) * weight) * taylor[k, :, lane(f)]
            slow[:, lane(f)] = total

    loads[2].wait()
    for chunk in chunks:
        value = side_by_side([out_ref[f] for f in chunk])
        part[:, cols(chunk)] = value
        y_even[:, cols(chunk)] = stiff_rows(value)
    loads[3].wait()

    weight = 1.0
    source, target = y_even, y_odd
    for k in range(DEGREE - 1):
        weight = weight / (k + 2)
        for chunk in chunks:
            value = side_by_side(contract(source, fields, star_ref, chunk))
            taylor[k, :, cols(chunk)] = value
            part[:, cols(chunk)] = part[:, cols(chunk)] + weight * value
            target[:, cols(chunk)] = stiff_rows(value)
        source, target = target, source
    weight = weight / (DEGREE + 1)
    loads[4].wait()
    proj_w[...] = columns3(by_face(proj_ref), depth)
    for chunk in chunks:
        value = side_by_side(contract(source, fields, star_ref, chunk))
        taylor[DEGREE - 1, :, cols(chunk)] = value
        value = part[:, cols(chunk)] + weight * value
        part[:, cols(chunk)] = value
        project(chunk, value)
    send_traces(0)

    for load in loads[5:]:
        load.wait()
    prepare_update()
    own_update()
    prepare_pairs()
    sum_slow()
    take_arrivals(0)
    near_update()
    finish_sends(0)

    for chunk in pair_chunks:
        value = []
        for i in chunk:
            first = out_ref[2 * i]
            second = out_ref[min(2 * i + 1, fields - 1)]
            value.append(pair_up(first, second))
        value = side_by_side(value)
        part_pair[:, cols(chunk)] = value
        pair_even[:, cols(chunk)] = stiff_rows(value)

    weight = 1.0
    source, target = pair_even, pair_odd
    for k in range(DEGREE - 1):
        weight = weight / (k + 2)
        for chunk in pair_chunks:
            value = contract_pairs(source, chunk)
            part_pair[:, cols(chunk)] = part_pair[:, cols(chunk)] + weight * value
            target[:, cols(chunk)] = stiff_rows(value)
        source, target = target, source
    weight = weight / (DEGREE + 1)
    is_fast = lax.broadcasted_iota(jnp.int32, (modes, LANES), 1) < count_ref[0]
    for chunk in pair_chunks:
        value = part_pair[:, cols(chunk)] + weight * contract_pairs(source, chunk)
        for n, i in enumerate(chunk):
            item = value[:, lane(n)]
            both = [item, pltpu.roll(item, half, 1)]
            mine = tuple(f for f in (2 * i, 2 * i + 1) if f < fields)
            mixed = [
                jnp.where(is_fast, both[q], slow[:, lane(f)]) for q, f in enumerate(mine)
            ]
            project(mine, side_by_side(mixed))
    send_traces(1)
    own_update()
    take_arrivals(1)
    near_update()
    finish_sends(1)


def local(
    n_dom,
    n_sub,
    modal_state,
    star_mats,
    face_flux,
    stiffness,
    stiff_vol,
    face_proj,
    face_lifting_matrix,
    orient_maps,
    neighbours,
    face_orient,
    send_slots,
    fast_count,
):
    modes, fields, elems = modal_state.shape
    face_modes = orient_maps.shape[1]
    slots = send_slots.shape[1]
    fold = LANES // slots
    face_pad, mode_pad = up(face_modes, 8), up(modes, 16)
    table_rows = up((fields - 1) * face_modes + face_pad, 8 * fold)
    group = n_sub * slots
    width = fields * elems
    pairs = (fields + 1) // 2
    depth, rows3 = up(3 * modes, 16), up(3 * modes, 16)
    face_rows = 4 * face_pad
    any_space = pl.BlockSpec(memory_space=pl.ANY)
    vmem = pl.BlockSpec(memory_space=pltpu.VMEM)
    out = pl.pallas_call(
        functools.partial(kernel, (n_dom, n_sub, modes, fields, face_pad, slots)),
        out_shape=pltpu.VMEM((fields, modes, elems), F32),
        in_specs=[any_space] * 11 + [pl.BlockSpec(memory_space=pltpu.SMEM)],
        out_specs=vmem,
        scratch_shapes=[
            pltpu.VMEM(neighbours.shape, jnp.int32),
            pltpu.VMEM(face_orient.shape, jnp.int32),
            pltpu.VMEM(send_slots.shape, jnp.int32),
            pltpu.VMEM((fields, fields, 3, elems), F32),
            pltpu.VMEM((2, fields, fields, 4, elems), F32),
            pltpu.VMEM((3, modes, modes), F32),
            pltpu.VMEM((3, modes, modes), F32),
            pltpu.VMEM((face_modes, 4, modes), F32),
            pltpu.VMEM((face_modes, 4, modes), F32),
            pltpu.VMEM((3, face_modes, face_modes), F32),
            pltpu.SemaphoreType.DMA((11,)),
            pltpu.VMEM((fields, pairs, 3, elems), F32),
            pltpu.VMEM((3 * modes, width), F32),
            pltpu.VMEM((3 * modes, width), F32),
            pltpu.VMEM((3 * modes, pairs * elems), F32),
            pltpu.VMEM((3 * modes, pairs * elems), F32),
            pltpu.VMEM((modes, width), F32),
            pltpu.VMEM((modes, pairs * elems), F32),
            pltpu.VMEM((DEGREE, modes, width), F32),
            pltpu.VMEM((modes, width), F32),
            pltpu.VMEM((depth, width), BF16),
            pltpu.VMEM((4, table_rows, elems), F32),
            pltpu.VMEM((table_rows, 8 * elems), BF16),
            pltpu.VMEM((4, table_rows, elems), F32),
            pltpu.VMEM((table_rows, 6 * group), BF16),
            pltpu.VMEM((rows3, depth), BF16),
            pltpu.VMEM((rows3, depth), BF16),
            pltpu.VMEM((face_rows, depth), BF16),
            pltpu.VMEM((mode_pad, 3 * face_rows), BF16),
            pltpu.VMEM((2, mode_pad, 9 * face_rows // 2), BF16),
            pltpu.VMEM((4 * elems, 4 * elems), BF16),
            pltpu.VMEM((3 * group, 4 * elems), BF16),
            pltpu.VMEM((4 * elems, 2 * LANES), BF16),
            pltpu.VMEM((3, face_rows, LANES), F32),
            pltpu.VMEM((2, 2, table_rows // fold, LANES), F32),
            pltpu.VMEM((2, 3, n_sub, table_rows // fold, LANES), F32),
            pltpu.SemaphoreType.DMA((2, 3, n_sub)),
            pltpu.SemaphoreType.DMA((2, 3, n_sub)),
            pltpu.SemaphoreType.DMA((2, 3, n_sub)),
        ],
        compiler_params=pltpu.CompilerParams(collective_id=0, has_side_effects=True),
    )(
        modal_state.transpose(1, 0, 2),
        star_mats.transpose(1, 2, 0, 3),
        face_flux.transpose(0, 2, 3, 1, 4),
        stiffness,
        stiff_vol,
        face_proj.transpose(2, 0, 1),
        face_lifting_matrix.transpose(1, 0, 2),
        orient_maps,
        neighbours,
        face_orient,
        send_slots,
        fast_count,
    )
    return out.transpose(1, 0, 2)


def solution(mesh):
    split_last = ("dom", "sub")
    placed = (
        P(None, None, split_last),
        P(None, None, None, split_last),
        P(None, None, None, None, split_last),
        P(),
        P(),
        P(),
        P(),
        P(),
        P(None, split_last),
        P(None, split_last),
        P(None, split_last),
        P(split_last),
    )
    return jax.shard_map(
        functools.partial(local, mesh.shape["dom"], mesh.shape["sub"]),
        mesh=mesh,
        in_specs=placed,
        out_specs=P(None, None, split_last),
        check_vma=False,
    )
```

```python
import functools

import jax
import jax.numpy as jnp
from jax import lax
from jax.experimental import pallas as pl
from jax.experimental.pallas import tpu as pltpu
from jax.sharding import PartitionSpec as P

DEGREE = 5
LANES = 128
F32 = jnp.float32
BF16 = jnp.bfloat16


def up(value, multiple):
    return -(-value // multiple) * multiple


def split(x):
    hi = x.astype(BF16)
    return hi, (x - hi.astype(F32)).astype(BF16)


def stacked(x):
    hi, lo = split(x)
    return jnp.concatenate([hi, lo], axis=0)


def dot(a, b):
    return jnp.dot(a, b, preferred_element_type=F32)


def rows3(x, depth):
    low = x - x.astype(BF16).astype(F32)
    rest = depth - 3 * x.shape[0]
    parts = [x, low, x]
    if rest:
        parts.append(jnp.zeros((rest, x.shape[1]), F32))
    return jnp.concatenate(parts, axis=0).astype(BF16)


def twice(x):
    return jnp.concatenate([x, x], axis=0)


def grow(x, rows):
    if rows == x.shape[0]:
        return x
    return jnp.concatenate([x, jnp.zeros((rows - x.shape[0], x.shape[1]), F32)], axis=0)


def row_of(ref, *lead_and_row):
    lead, row = lead_and_row[:-1], lead_and_row[-1]
    return ref[(*lead, pl.ds(row, 1), slice(None))]


def at_columns(rows, columns, test):
    row = lax.broadcasted_iota(jnp.int32, (rows, columns), 0)
    column = lax.broadcasted_iota(jnp.int32, (rows, columns), 1)
    return jnp.where(test(row, column), 1.0, 0.0).astype(BF16)


def shifted(rows, columns, shift):
    return at_columns(rows, columns, lambda row, column: column == row + shift)


def columns3(w, depth):
    hi, lo = split(w)
    inner = w.shape[1]
    first = at_columns(inner, depth, lambda r, c: (c == r) | (c == r + inner))
    return (dot(hi, first) + dot(lo, shifted(inner, depth, 2 * inner))).astype(BF16)


def kernel(
    sizes,
    state_hbm,
    star_hbm,
    flux_hbm,
    stiff_hbm,
    vol_hbm,
    proj_hbm,
    lift_hbm,
    maps_hbm,
    near_idx_hbm,
    orient_hbm,
    slots_hbm,
    count_ref,
    out_ref,
    near_idx_ref,
    orient_ref,
    slots_ref,
    star_ref,
    flux_ref,
    stiff_ref,
    vol_ref,
    proj_ref,
    lift_ref,
    maps_ref,
    load_sem,
    star_pair,
    y_even,
    y_odd,
    pair_even,
    pair_odd,
    part,
    part_pair,
    taylor,
    slow,
    part_rows,
    trace,
    table,
    near,
    remote,
    pred_w,
    vol_w,
    proj_w,
    own_w,
    near_w,
    hot_local,
    hot_remote,
    hot_send,
    mask,
    send,
    recv,
    send_sem,
    recv_sem,
    forward_sem,
):
    n_dom, n_sub, modes, fields, face_pad, slots = sizes
    faces = 4
    face_modes = maps_ref.shape[1]
    half = LANES // 2
    pairs = (fields + 1) // 2
    depth = pred_w.shape[1]
    mode_pad = up(modes, 16)
    fold = LANES // slots
    table_rows = table.shape[0]
    fold_rows = table_rows // fold
    group = n_sub * slots
    face_rows = faces * face_pad
    own_count = faces * LANES
    loads = [
        pltpu.make_async_copy(source, target, load_sem.at[i])
        for i, (source, target) in enumerate(
            [
                (slots_hbm, slots_ref),
                (stiff_hbm, stiff_ref),
                (state_hbm, out_ref),
                (star_hbm, star_ref),
                (proj_hbm, proj_ref),
                (vol_hbm, vol_ref),
                (lift_hbm, lift_ref),
                (maps_hbm, maps_ref),
                (flux_hbm, flux_ref),
                (near_idx_hbm, near_idx_ref),
                (orient_hbm, orient_ref),
            ]
        )
    ]
    for load in loads:
        load.start()
    dom, sub = lax.axis_index("dom"), lax.axis_index("sub")
    has_low, has_high = dom > 0, dom < n_dom - 1

    barrier = pltpu.get_barrier_semaphore()

    def greet(d, s):
        pl.semaphore_signal(
            barrier, inc=1, device_id={"dom": d, "sub": s}, device_id_type=pl.DeviceIdType.MESH
        )

    chips = n_sub // 2
    chip, core = sub // 2, lax.rem(sub, 2)
    sibling = 2 * chip + 1 - core

    greet(dom, sibling)
    for k in range(1, chips):
        greet(dom, 2 * lax.rem(chip + k, chips) + core)

    @pl.when(has_low)
    def _():
        for c in range(chips):
            greet(dom - 1, 2 * c + core)

    @pl.when(has_high)
    def _():
        for c in range(chips):
            greet(dom + 1, 2 * c + core)

    @pl.when(jnp.logical_not(has_low))
    def _():
        recv[:, 1] = jnp.zeros((2, *recv.shape[2:]), F32)

    @pl.when(jnp.logical_not(has_high))
    def _():
        recv[:, 2] = jnp.zeros((2, *recv.shape[2:]), F32)

    def one_hot(row, rows):
        at = lax.broadcasted_iota(jnp.int32, (rows, LANES), 0)
        return jnp.where(at == row, 1.0, 0.0).astype(BF16)

    loads[0].wait()
    tiled = dot(
        stacked(grow(slots_ref[...].astype(F32), 8)),
        at_columns(slots, LANES, lambda row, column: column % slots == row),
    )
    tiled = (tiled[:8] + tiled[8:]).astype(jnp.int32)
    for i in range(2):
        hot_send[:, i * LANES : (i + 1) * LANES] = one_hot(tiled[i : i + 1, :], own_count)

    def by_direction(ref):
        rows = jnp.concatenate([ref[d] for d in range(3)], axis=0)
        return grow(rows, pred_w.shape[0])

    def by_face(ref):
        return jnp.concatenate([grow(ref[:, j, :], face_pad) for j in range(faces)], axis=0)

    loads[1].wait()
    pred_w[...] = columns3(-by_direction(stiff_ref), depth)

    chunks = [tuple(range(f, min(f + 2, fields))) for f in range(0, fields, 2)]
    pair_chunks = [tuple(range(i, min(i + 2, pairs))) for i in range(0, pairs, 2)]

    def cols(chunk):
        return slice(chunk[0] * LANES, (chunk[-1] + 1) * LANES)

    def lane(i):
        return slice(i * LANES, (i + 1) * LANES)

    def side_by_side(values):
        return values[0] if len(values) == 1 else jnp.concatenate(values, axis=1)

    def stiff_rows(value):
        return dot(pred_w[...], rows3(value, depth))[: 3 * modes]

    def contract(source, terms, rows, targets, size, sums):
        values = [[] for _ in targets]
        for start in range(0, modes, size):
            count = min(size, modes - start)
            totals = [[None] * sums for _ in targets]
            for g in range(terms):
                for d in range(3):
                    first = d * modes + start
                    item = source[first : first + count, lane(g)]
                    for i, f in enumerate(targets):
                        term = row_of(rows, f, g, d) * item
                        total = totals[i][d % sums]
                        totals[i][d % sums] = term if total is None else total + term
            for i, total in enumerate(totals):
                values[i].append(functools.reduce(jnp.add, total))
        return [jnp.concatenate(value, axis=0) for value in values]

    low_half = lax.broadcasted_iota(jnp.int32, (modes, LANES), 1) < half

    def pair_up(first, second):
        return jnp.where(low_half, first, pltpu.roll(second, half, 1))

    def contract_pairs(source, chunk):
        targets = [f for i in chunk for f in (2 * i, 2 * i + 1) if f < fields]
        values = contract(source, pairs, star_pair, targets, 56, 1)
        if len(targets) < 2 * len(chunk):
            values.append(jnp.zeros((modes, LANES), F32))
        result = []
        for i in range(len(chunk)):
            even, odd = values[2 * i], values[2 * i + 1]
            result.append(
                jnp.where(low_half, even, odd)
                + pltpu.roll(jnp.where(low_half, odd, even), half, 1)
            )
        return side_by_side(result)

    def project(chunk, value):
        rows = rows3(value, depth)
        part_rows[:, cols(chunk)] = rows
        value = dot(proj_w[...], rows)
        for i, g in enumerate(chunk):
            for j in range(faces):
                trace[j, g * face_modes : g * face_modes + face_pad, :] = value[
                    j * face_pad : (j + 1) * face_pad, lane(i)
                ]

    def flux_rows(side, src, chunk, of=range(faces)):
        found = [[] for _ in chunk]
        for j in of:
            totals = [None] * len(chunk)
            for g in range(fields):
                item = src[j, g * face_modes : g * face_modes + face_pad, :]
                for i, f in enumerate(chunk):
                    term = row_of(flux_ref, side, f, g, j) * item
                    totals[i] = term if totals[i] is None else totals[i] + term
            for i, total in enumerate(totals):
                found[i].append(total)
        return [jnp.concatenate(value, axis=0) for value in found]

    def add_out(chunk, value):
        for i, f in enumerate(chunk):
            out_ref[f] = out_ref[f] + value[:modes, lane(i)]

    def out_copy(ex, which, target, region, at):
        return pltpu.make_async_remote_copy(
            src_ref=send.at[ex, which],
            dst_ref=recv.at[ex, region, sub],
            send_sem=send_sem.at[region, at],
            recv_sem=recv_sem.at[ex, region, sub],
            device_id=target,
            device_id_type=pl.DeviceIdType.MESH,
        )

    def exchange_copies(ex):
        inner = [out_copy(ex, 0, {"dom": dom, "sub": sibling}, 0, 0)]
        for k in range(1, chips):
            target = {"dom": dom, "sub": 2 * lax.rem(chip + k, chips) + core}
            inner.append(out_copy(ex, 0, target, 0, k))
        lower, upper = [], []
        for k in reversed(range(chips)):
            at = 2 * lax.rem(chip + k, chips) + core
            lower.append(out_copy(ex, 1, {"dom": dom - 1, "sub": at}, 2, k))
            upper.append(out_copy(ex, 1, {"dom": dom + 1, "sub": at}, 1, k))
        return inner, lower, upper

    def arrival(ex, region, s):
        return pltpu.make_async_remote_copy(
            src_ref=send.at[ex, 0],
            dst_ref=recv.at[ex, region, s],
            send_sem=send_sem.at[region, 0],
            recv_sem=recv_sem.at[ex, region, s],
            device_id={"dom": dom, "sub": sub},
            device_id_type=pl.DeviceIdType.MESH,
        )

    def forward(ex, region, s):
        return pltpu.make_async_remote_copy(
            src_ref=recv.at[ex, region, s],
            dst_ref=recv.at[ex, region, s],
            send_sem=forward_sem.at[region, s // 2],
            recv_sem=recv_sem.at[ex, region, s],
            device_id={"dom": dom, "sub": sibling},
            device_id_type=pl.DeviceIdType.MESH,
        )

    def each_region(do, side):
        for k in range(1, chips):
            do(0, 2 * lax.rem(chip + k, chips) + side)
        for k in range(chips):
            at = 2 * lax.rem(chip + k, chips) + side

            @pl.when(has_low)
            def _():
                do(1, at)

            @pl.when(has_high)
            def _():
                do(2, at)

    section = lax.broadcasted_iota(jnp.int32, (fold_rows, LANES), 1) // slots

    def send_traces(ex):
        picked = []
        for a in range(0, fold, 2):
            rows = slice(a * fold_rows, (a + 2) * fold_rows)
            for j in range(faces):
                hi, lo = split(trace[j, rows, :])
                table[rows, lane(j)] = hi
                table[rows, lane(faces + j)] = lo
            found = dot(table[rows, :], twice(hot_send[...]))
            picked += [found[:fold_rows], found[fold_rows:]]
        for i in range(2):
            packed = picked[0][:, lane(i)]
            for a in range(1, fold):
                packed = jnp.where(section == a, picked[a][:, lane(i)], packed)
            send[ex, i] = packed
            if i == 0:
                recv[ex, 0, sub] = packed
        if ex == 0:
            pl.semaphore_wait(
                barrier, chips * (1 + has_low.astype(jnp.int32) + has_high.astype(jnp.int32))
            )
        inner, lower, upper = exchange_copies(ex)

        @pl.when(has_low)
        def _():
            for copy in lower:
                copy.start()

        @pl.when(has_high)
        def _():
            for copy in upper:
                copy.start()

        for copy in inner:
            copy.start()

    def own_update():
        for jj in range(0, faces, 2):
            at = slice(jj * LANES, (jj + 2) * LANES)
            found = dot(table[...], twice(hot_local[:, at]))
            near[jj] = found[:, :LANES]
            near[jj + 1] = found[:, LANES:]
        for chunk in chunks:
            y_even[:, cols(chunk)] = dot(vol_w[...], part_rows[:, cols(chunk)])[: 3 * modes]
        for chunk in chunks:
            volume = side_by_side(contract(y_even, fields, star_ref, chunk, 16, 3))
            own = side_by_side(flux_rows(0, trace, chunk))
            add_out(chunk, volume + dot(own_w[...], rows3(own, 3 * face_rows))[:modes])

    def take_arrivals(ex):
        def pass_on(region, s):
            arrival(ex, region, s).wait_recv()
            forward(ex, region, s).start()

        each_region(pass_on, core)
        arrival(ex, 0, sibling).wait_recv()
        each_region(lambda region, s: arrival(ex, region, s).wait_recv(), 1 - core)

        for region in range(3):
            for b in range(n_sub // fold):
                parts = [recv[ex, region, b * fold + i] for i in range(fold)]
                turned = []
                for shift in range(fold):
                    value = parts[shift]
                    for a in range(1, fold):
                        value = jnp.where(section == a, parts[(a + shift) % fold], value)
                    if shift:
                        value = pltpu.roll(value, shift * slots, 1)
                    turned.append(value)
                for a in range(fold):
                    value = turned[-a % fold]
                    for i in range(1, fold):
                        value = jnp.where(section == i, turned[(i - a) % fold], value)
                    first = region * group + b * LANES
                    rows = slice(a * fold_rows, (a + 1) * fold_rows)
                    hi, lo = split(value)
                    remote[rows, first : first + LANES] = hi
                    first = first + 3 * group
                    remote[rows, first : first + LANES] = lo

    def near_update():
        for jj in range(0, faces, 2):
            at = slice(jj * LANES, (jj + 2) * LANES)
            found = dot(remote[...], twice(hot_remote[:, at]))
            near[jj] = near[jj] + found[:, :LANES]
            near[jj + 1] = near[jj + 1] + found[:, LANES:]
        for jj in range(0, faces, 2):
            rows = slice(jj * face_pad, (jj + 2) * face_pad)
            masks = [mask[o, rows, :].astype(BF16) for o in range(3)]
            for chunk in chunks:
                pieces = []
                for value in flux_rows(1, near, chunk, (jj, jj + 1)):
                    hi, lo = split(value)
                    hi = [hi * masks[o] for o in range(3)]
                    lo = [lo * masks[o] for o in range(3)]
                    pieces.append(jnp.concatenate(hi + lo + hi, axis=0))
                add_out(chunk, dot(near_w[jj // 2], side_by_side(pieces)))

    def finish_sends(ex):
        inner, lower, upper = exchange_copies(ex)
        for copy in inner:
            copy.wait_send()

        @pl.when(has_low)
        def _():
            for copy in lower:
                copy.wait_send()

        @pl.when(has_high)
        def _():
            for copy in upper:
                copy.wait_send()

        each_region(lambda region, s: forward(ex, region, s).wait_send(), core)

    def prepare_update():
        for j in range(faces):
            row = near_idx_ref[j : j + 1, :]
            hot_local[:, lane(j)] = one_hot(row, own_count)
            hot_remote[:, lane(j)] = one_hot(row - own_count, 3 * group)
            turn = orient_ref[j : j + 1, :]
            for o in range(3):
                mask[o, j * face_pad : (j + 1) * face_pad, :] = jnp.broadcast_to(
                    jnp.where(turn == o, 1.0, 0.0), (face_pad, LANES)
                )
        vol_w[...] = columns3(by_direction(vol_ref), depth)
        same = shifted(mode_pad, modes, 0)
        lift = []
        for value in split(-by_face(lift_ref)):
            lift.append(
                lax.dot_general(same, value, (((1,), (1,)), ((), ())), preferred_element_type=F32)
            )
        hi, lo = lift[0].astype(BF16), lift[1].astype(BF16)
        own_w[:, :face_rows] = hi
        own_w[:, face_rows : 2 * face_rows] = hi
        own_w[:, 2 * face_rows :] = lo
        map_pad = up(face_pad, 16)
        pair_rows = 2 * face_pad
        maps = [stacked(grow(maps_ref[o], map_pad)) for o in range(3)]
        for jj in range(0, faces, 2):
            turned = None
            for o in range(3):
                place = at_columns(
                    face_modes,
                    3 * pair_rows,
                    lambda row, column: (column // pair_rows == o) & (column % face_pad == row),
                )
                both = dot(maps[o], place)
                term = both[:face_pad] + both[map_pad : map_pad + face_pad]
                turned = term if turned is None else turned + term
            turned = jnp.concatenate([turned] * faces, axis=0)
            row = lax.broadcasted_iota(jnp.int32, turned.shape, 0)
            column = lax.broadcasted_iota(jnp.int32, turned.shape, 1)
            same_face = column % pair_rows // face_pad + jj == row // face_pad
            turned_hi, turned_lo = split(jnp.where(same_face, turned, 0.0))
            value = dot(hi, turned_hi) + dot(lo, turned_hi) + dot(hi, turned_lo)
            value_hi, value_lo = split(value)
            near_w[jj // 2, :, : 3 * pair_rows] = value_hi
            near_w[jj // 2, :, 3 * pair_rows : 6 * pair_rows] = value_hi
            near_w[jj // 2, :, 6 * pair_rows :] = value_lo

    def prepare_pairs():
        low = lax.broadcasted_iota(jnp.int32, (8, LANES), 1) < half
        for f in range(fields):
            for i in range(pairs):
                first = grow(star_ref[f, 2 * i], 8)
                if 2 * i + 1 < fields:
                    second = pltpu.roll(grow(star_ref[f, 2 * i + 1], 8), half, 1)
                else:
                    second = jnp.zeros((8, LANES), F32)
                star_pair[f, i] = jnp.where(low, first, second)[:3]

    def sum_slow():
        for f in range(fields):
            total = part[:, lane(f)]
            weight = 1.0
            for k in range(DEGREE):
                weight = weight / (k + 2)
                total = total + ((2.0 ** (k + 2) - 2.0) * weight) * taylor[k, :, lane(f)]
            slow[:, lane(f)] = total

    loads[2].wait()
    for chunk in chunks:
        value = side_by_side([out_ref[f] for f in chunk])
        part[:, cols(chunk)] = value
        y_even[:, cols(chunk)] = stiff_rows(value)
    loads[3].wait()
    loads[4].wait()
    proj_w[...] = columns3(by_face(proj_ref), depth)

    weight = 1.0
    source, target = y_even, y_odd
    for k in range(DEGREE - 1):
        weight = weight / (k + 2)
        for chunk in chunks:
            value = side_by_side(contract(source, fields, star_ref, chunk, 16, 3))
            taylor[k, :, cols(chunk)] = value
            part[:, cols(chunk)] = part[:, cols(chunk)] + weight * value
            target[:, cols(chunk)] = stiff_rows(value)
        source, target = target, source
    weight = weight / (DEGREE + 1)
    for chunk in chunks:
        value = side_by_side(contract(source, fields, star_ref, chunk, 16, 3))
        taylor[DEGREE - 1, :, cols(chunk)] = value
        value = part[:, cols(chunk)] + weight * value
        part[:, cols(chunk)] = value
        project(chunk, value)
    send_traces(0)

    for load in loads[5:]:
        load.wait()
    prepare_update()
    own_update()
    prepare_pairs()
    sum_slow()
    take_arrivals(0)
    near_update()
    finish_sends(0)

    for chunk in pair_chunks:
        value = []
        for i in chunk:
            first = out_ref[2 * i]
            second = out_ref[min(2 * i + 1, fields - 1)]
            value.append(pair_up(first, second))
        value = side_by_side(value)
        part_pair[:, cols(chunk)] = value
        pair_even[:, cols(chunk)] = stiff_rows(value)

    weight = 1.0
    source, target = pair_even, pair_odd
    for k in range(DEGREE - 1):
        weight = weight / (k + 2)
        for chunk in pair_chunks:
            value = contract_pairs(source, chunk)
            part_pair[:, cols(chunk)] = part_pair[:, cols(chunk)] + weight * value
            target[:, cols(chunk)] = stiff_rows(value)
        source, target = target, source
    weight = weight / (DEGREE + 1)
    is_fast = lax.broadcasted_iota(jnp.int32, (modes, LANES), 1) < count_ref[0]
    for chunk in pair_chunks:
        value = part_pair[:, cols(chunk)] + weight * contract_pairs(source, chunk)
        for n, i in enumerate(chunk):
            item = value[:, lane(n)]
            both = [item, pltpu.roll(item, half, 1)]
            mine = tuple(f for f in (2 * i, 2 * i + 1) if f < fields)
            mixed = [
                jnp.where(is_fast, both[q], slow[:, lane(f)]) for q, f in enumerate(mine)
            ]
            project(mine, side_by_side(mixed))
    send_traces(1)
    own_update()
    take_arrivals(1)
    near_update()
    finish_sends(1)


def local(
    n_dom,
    n_sub,
    modal_state,
    star_mats,
    face_flux,
    stiffness,
    stiff_vol,
    face_proj,
    face_lifting_matrix,
    orient_maps,
    neighbours,
    face_orient,
    send_slots,
    fast_count,
):
    modes, fields, elems = modal_state.shape
    face_modes = orient_maps.shape[1]
    slots = send_slots.shape[1]
    fold = LANES // slots
    face_pad, mode_pad = up(face_modes, 8), up(modes, 16)
    table_rows = up((fields - 1) * face_modes + face_pad, 8 * fold)
    group = n_sub * slots
    width = fields * elems
    pairs = (fields + 1) // 2
    depth, rows3 = up(3 * modes, 16), up(3 * modes, 16)
    face_rows = 4 * face_pad
    any_space = pl.BlockSpec(memory_space=pl.ANY)
    vmem = pl.BlockSpec(memory_space=pltpu.VMEM)
    out = pl.pallas_call(
        functools.partial(kernel, (n_dom, n_sub, modes, fields, face_pad, slots)),
        out_shape=pltpu.VMEM((fields, modes, elems), F32),
        in_specs=[any_space] * 11 + [pl.BlockSpec(memory_space=pltpu.SMEM)],
        out_specs=vmem,
        scratch_shapes=[
            pltpu.VMEM(neighbours.shape, jnp.int32),
            pltpu.VMEM(face_orient.shape, jnp.int32),
            pltpu.VMEM(send_slots.shape, jnp.int32),
            pltpu.VMEM((fields, fields, 3, elems), F32),
            pltpu.VMEM((2, fields, fields, 4, elems), F32),
            pltpu.VMEM((3, modes, modes), F32),
            pltpu.VMEM((3, modes, modes), F32),
            pltpu.VMEM((face_modes, 4, modes), F32),
            pltpu.VMEM((face_modes, 4, modes), F32),
            pltpu.VMEM((3, face_modes, face_modes), F32),
            pltpu.SemaphoreType.DMA((11,)),
            pltpu.VMEM((fields, pairs, 3, elems), F32),
            pltpu.VMEM((3 * modes, width), F32),
            pltpu.VMEM((3 * modes, width), F32),
            pltpu.VMEM((3 * modes, pairs * elems), F32),
            pltpu.VMEM((3 * modes, pairs * elems), F32),
            pltpu.VMEM((modes, width), F32),
            pltpu.VMEM((modes, pairs * elems), F32),
            pltpu.VMEM((DEGREE, modes, width), F32),
            pltpu.VMEM((modes, width), F32),
            pltpu.VMEM((depth, width), BF16),
            pltpu.VMEM((4, table_rows, elems), F32),
            pltpu.VMEM((table_rows, 8 * elems), BF16),
            pltpu.VMEM((4, table_rows, elems), F32),
            pltpu.VMEM((table_rows, 6 * group), BF16),
            pltpu.VMEM((rows3, depth), BF16),
            pltpu.VMEM((rows3, depth), BF16),
            pltpu.VMEM((face_rows, depth), BF16),
            pltpu.VMEM((mode_pad, 3 * face_rows), BF16),
            pltpu.VMEM((2, mode_pad, 9 * face_rows // 2), BF16),
            pltpu.VMEM((4 * elems, 4 * elems), BF16),
            pltpu.VMEM((3 * group, 4 * elems), BF16),
            pltpu.VMEM((4 * elems, 2 * LANES), BF16),
            pltpu.VMEM((3, face_rows, LANES), F32),
            pltpu.VMEM((2, 2, table_rows // fold, LANES), F32),
            pltpu.VMEM((2, 3, n_sub, table_rows // fold, LANES), F32),
            pltpu.SemaphoreType.DMA((3, n_sub // 2)),
            pltpu.SemaphoreType.DMA((2, 3, n_sub)),
            pltpu.SemaphoreType.DMA((3, n_sub // 2)),
        ],
        compiler_params=pltpu.CompilerParams(collective_id=0, has_side_effects=True),
    )(
        modal_state.transpose(1, 0, 2),
        star_mats.transpose(1, 2, 0, 3),
        face_flux.transpose(0, 2, 3, 1, 4),
        stiffness,
        stiff_vol,
        face_proj.transpose(2, 0, 1),
        face_lifting_matrix.transpose(1, 0, 2),
        orient_maps,
        neighbours,
        face_orient,
        send_slots,
        fast_count,
    )
    return out.transpose(1, 0, 2)


def solution(mesh):
    split_last = ("dom", "sub")
    placed = (
        P(None, None, split_last),
        P(None, None, None, split_last),
        P(None, None, None, None, split_last),
        P(),
        P(),
        P(),
        P(),
        P(),
        P(None, split_last),
        P(None, split_last),
        P(None, split_last),
        P(split_last),
    )
    return jax.shard_map(
        functools.partial(local, mesh.shape["dom"], mesh.shape["sub"]),
        mesh=mesh,
        in_specs=placed,
        out_specs=P(None, None, split_last),
        check_vma=False,
    )
```
